256 devices in a mesh: row: 32 (over z, y_hi, core), col: 8 (over x, y_lo).
Axes of the slice: x: 4, y: 4 (y_hi: 2, y_lo: 2; y = y_hi * 2 + y_lo), z: 8, core: 2. Of those that a mesh axis runs over, the one named last changes fastest.
Arguments:
- matrix: float32 [32, 8, 64, 4, 32, 128], P(None, 'col', None, None, 'row'), may hold values from -6 to 128, as said below
- column_weight: float32 [4, 32, 128], P(None, 'row'), may hold values from -0.046875 to 0.046875
- row_weight: float32 [32, 8, 64], P(None, 'col'), may hold values from -0.046875 to 0.046875
Outputs:
- factored: float32 [32, 8, 64, 4, 32, 128], P(None, 'col', None, None, 'row')
- row_checks: float32 [32, 8, 64], P(None, 'col')
- column_checks: float32 [4, 32, 128], P(None, 'row')
The draws below stay inside these ranges and needn't reach their ends.
Inputs may be any that keep to these rules, and one draw needn't show every extreme that they name: `matrix`: the diagonal entries lie between 64 and 128; every other entry has magnitude at most 6.
All inputs are finite; a program needn't handle non-finite values.
Results may differ from the reference program's by a relative error of at most 0.0003.
Values sent between devices are 32-bit elements; how exact they have to be, the bound alone decides.
A program may use at most 64 MiB of HBM per device.

```python
import jax
import jax.numpy as jnp
from jax import lax

N = 16384
PANEL = 64
RBLK = 32
CBLK = 4
N_ROW = 32
N_COL = 8


def draw_matrix(key, part):
    matrix_order = N
    key_noise = jax.random.fold_in(key, 11)
    key_diagonal = jax.random.fold_in(key, 23)
    spread_part = jnp.clip(jax.random.normal(key_noise, (matrix_order, matrix_order), jnp.float32), -6.0, 6.0)
    diagonal = jax.random.uniform(key_diagonal, (matrix_order,), jnp.float32, 64.0, 128.0)
    positions = jnp.arange(matrix_order)
    whole = spread_part.at[positions, positions].set(diagonal)
    return whole.reshape(RBLK, N_COL, PANEL, CBLK, N_ROW, 2 * PANEL)


def steps_of(key, dims, pieces, low, high):
    def one(axis_at, shards_of):
        draws = jax.random.uniform(jax.random.fold_in(jax.random.fold_in(key, 6), axis_at), (shards_of,), jnp.float32, low / len(pieces), high / len(pieces))
        return jnp.repeat(jnp.exp(draws), dims[axis_at] // shards_of).reshape((-1,) + (1,) * (len(dims) - axis_at - 1))

    factor_of = one(*pieces[0])
    for cut in pieces[1:]:
        factor_of = factor_of * one(*cut)
    return factor_of


def centred(stream_key, dims, scale, limit, cuts=(), kind=jnp.bfloat16):
    values = jax.random.normal(stream_key, dims, jnp.float32) * scale
    if len(cuts) > 0:
        values = steps_of(stream_key, dims, cuts, -0.22, 0.18) * values
    return jnp.clip(values, min=-limit, max=limit).astype(kind)


def setup_inputs(seed: int = 0) -> dict:
    seeds = jax.random.split(jax.random.key(seed), 4)
    matrix = draw_matrix(jax.random.fold_in(seeds[3], 71), 0)
    column_weight = centred(seeds[1], (CBLK, N_ROW, 2 * PANEL), N ** -0.5, 0.046875, ((1, 32),), jnp.float32)
    row_weight = centred(seeds[2], (RBLK, N_COL, PANEL), N ** -0.5, 0.046875, ((1, 8),), jnp.float32)
    return {"matrix": matrix, "column_weight": column_weight, "row_weight": row_weight}


highest = lax.Precision.HIGHEST


def product(left, right):
    return jnp.dot(left, right, precision=highest, preferred_element_type=jnp.float32)


def unit_inverse(nilpotent, identity, side_len):
    result = identity - nilpotent
    power = product(nilpotent, nilpotent)
    reach = 2
    while reach < side_len:
        result = product(result, identity + power)
        power = product(power, power)
        reach = reach * 2
    return result


def factor_small(square):
    side_len = square.shape[0]
    positions = jnp.arange(side_len)
    packed = square
    for pivot_at in range(side_len):
        column = packed[:, pivot_at]
        across = packed[pivot_at, :]
        below = positions > pivot_at
        ratios = jnp.where(below, column / packed[pivot_at, pivot_at], 0.0)
        beyond = below[:, None] & below[None, :]
        packed = packed - jnp.where(beyond, ratios[:, None] * across[None, :], 0.0)
        packed = packed.at[:, pivot_at].set(jnp.where(below, ratios, column))
    identity = jnp.eye(side_len, dtype=square.dtype)
    strict_low = jnp.where(positions[:, None] > positions[None, :], packed, 0.0)
    lower = strict_low + identity
    upper = jnp.where(positions[:, None] <= positions[None, :], packed, 0.0)
    lower_inv = unit_inverse(strict_low, identity, side_len)
    diag_vals = jnp.diagonal(packed)
    strict_up = jnp.where(positions[:, None] < positions[None, :], packed / diag_vals[:, None], 0.0)
    upper_inv = unit_inverse(strict_up, identity, side_len) / diag_vals[None, :]
    return lower, upper, lower_inv, upper_inv


def factor_parts(square):
    side_len = square.shape[0]
    if side_len <= 16:
        return factor_small(square)
    half = side_len // 2
    lower_a, upper_a, linv_a, uinv_a = factor_parts(square[:half, :half])
    left_low = product(square[half:, :half], uinv_a)
    right_up = product(linv_a, square[:half, half:])
    schur = square[half:, half:] - product(left_low, right_up)
    lower_b, upper_b, linv_b, uinv_b = factor_parts(schur)
    zeros = jnp.zeros((half, side_len - half), square.dtype)
    lower = jnp.block([[lower_a, zeros], [left_low, lower_b]])
    upper = jnp.block([[upper_a, right_up], [zeros.T, upper_b]])
    linv_off = -product(linv_b, product(left_low, linv_a))
    uinv_off = -product(uinv_a, product(right_up, uinv_b))
    lower_inv = jnp.block([[linv_a, zeros], [linv_off, linv_b]])
    upper_inv = jnp.block([[uinv_a, uinv_off], [zeros.T, uinv_b]])
    return lower, upper, lower_inv, upper_inv


def factor_block(square):
    lower, upper, lower_inv, upper_inv = factor_parts(square)
    side_len = square.shape[0]
    positions = jnp.arange(side_len)
    packed = jnp.where(positions[:, None] > positions[None, :], lower, upper)
    return packed, lower_inv, upper_inv


def reference(matrix, column_weight, row_weight):
    matrix_order = matrix.shape[0] * matrix.shape[1] * matrix.shape[2]
    entries = matrix.reshape(matrix_order, matrix_order)
    weights_across = column_weight.reshape(matrix_order)
    weights_down = row_weight.reshape(matrix_order)
    row_checks = product(entries, weights_across)
    column_checks = product(weights_down, entries)
    for step_index in range(2):
        first_col = step_index * PANEL
        end_col = first_col + PANEL
        packed, lower_inv, upper_inv = factor_block(entries[first_col:end_col, first_col:end_col])
        left_part = product(entries[end_col:, first_col:end_col], upper_inv)
        right_part = product(lower_inv, entries[first_col:end_col, end_col:])
        check_down = product(lower_inv, row_checks[first_col:end_col])
        check_across = product(column_checks[first_col:end_col], upper_inv)
        entries = entries.at[end_col:, end_col:].set(entries[end_col:, end_col:] - product(left_part, right_part))
        row_checks = row_checks.at[end_col:].set(row_checks[end_col:] - product(left_part, check_down))
        column_checks = column_checks.at[end_col:].set(column_checks[end_col:] - product(check_across, right_part))
        entries = entries.at[end_col:, first_col:end_col].set(left_part)
        entries = entries.at[first_col:end_col, end_col:].set(right_part)
        entries = entries.at[first_col:end_col, first_col:end_col].set(packed)
        row_checks = row_checks.at[first_col:end_col].set(check_down)
        column_checks = column_checks.at[first_col:end_col].set(check_across)
    return (entries.reshape(matrix.shape), row_checks.reshape(row_weight.shape), column_checks.reshape(column_weight.shape))
```

```python
import jax
import jax.numpy as jnp
from jax import lax
from jax.experimental import pallas as pl
from jax.experimental.pallas import tpu as pltpu
from jax.sharding import PartitionSpec as P

MESH = pl.DeviceIdType.MESH
highest = lax.Precision.HIGHEST
F32 = jnp.float32
BF16 = jnp.bfloat16
NZ = 8
CH = 8
STEPS = 8


def spread_lane(x, i):
    return jnp.broadcast_to(x[:, i : i + 1], (8, 128))


def eliminate(g_ref, inv_ref, rows_ref, low_ref):
    lane = lax.broadcasted_iota(jnp.int32, (8, 128), 1)
    sub = lax.broadcasted_iota(jnp.int32, (8, 128), 0)
    low_ref[...] = jnp.zeros((128, 128), F32)

    def strip(s, vs):
        vs = list(vs)
        cols = [jnp.zeros((8, 128), F32)] * 16
        kept = jnp.zeros((8, 128), F32)
        for i in range(8):
            row = jnp.broadcast_to(vs[0][i : i + 1, :], (8, 128))
            here = lane == i
            recip = 1.0 / spread_lane(row, i)
            scaled = jnp.where(here, recip, row * recip)
            kept = jnp.where(sub == i, row, kept)
            for j in range(16):
                new = jnp.where(here, 0.0, vs[j]) - spread_lane(vs[j], i) * scaled
                cols[j] = jnp.where(here, -new, cols[j])
                if j == 0:
                    new = jnp.where(sub == i, scaled, new)
                vs[j] = new
        turn = s * 8
        rows_ref[pl.ds(pl.multiple_of(turn, 8), 8), :] = pltpu.roll(kept, turn, 1)
        for j in range(16):
            at = pl.multiple_of(lax.rem(s + j, 16) * 8, 8)
            low_ref[pl.ds(at, 8), :] += pltpu.roll(
                jnp.where(lane < 8, cols[j], 0.0), turn, 1
            )
        return tuple(pltpu.roll(x, 120, 1) for x in vs[1:] + vs[:1])

    out = lax.fori_loop(
        0, 16, strip, tuple(g_ref[8 * j : 8 * j + 8, :] for j in range(16))
    )
    for j in range(16):
        inv_ref[8 * j : 8 * j + 8, :] = out[j]


def exchange(
    a_hbm, w_hbm, v_hbm,
    p_ref, t_ref, inv_ref, rows_ref, low_ref, r_ref, rk_ref, c_ref,
    a_ref, w_ref, v_ref, rq_ref, rz_ref, rs_ref, cz_ref,
    load_sem, t_send, t_recv, own_recv, sib_recv, y_recv, rel_recv,
    dn_send, dn2_send, sib_send, y_send, rel_send, root_send,
    rq_send, rq_recv, rz_send, rz_recv, rg_send, rg_recv, rk_send, rk_recv,
    c_send, c_recv, i_send, i_recv, l_send, l_recv,
):
    me = lax.axis_index("row")
    col = lax.axis_index("col")
    z = me // 4
    q = lax.rem(me, 4)
    is_root = me == 0
    heads = col < 2

    def at_row(r):
        return dict(row=r, col=col)

    z_peers = [at_row(lax.rem(z + d, NZ) * 4 + q) for d in range(1, NZ)]
    q_peers = [at_row(z * 4 + lax.rem(q + d, 4)) for d in range(1, 4)]
    c_peers = [dict(row=me, col=lax.rem(col + d, 8)) for d in range(1, 8)]
    sib = at_row(z * 4 + (q + 1 - 2 * lax.rem(q, 2)))
    opp = at_row(z * 4 + lax.rem(q + 2, 4))

    loads = [
        pltpu.make_async_copy(a_hbm.at[:, b, :], a_ref.at[b], load_sem.at[b])
        for b in range(4)
    ]
    loads.append(pltpu.make_async_copy(w_hbm, w_ref, load_sem.at[4]))
    loads.append(pltpu.make_async_copy(v_hbm, v_ref, load_sem.at[5]))
    for x in loads:
        x.start()
    barrier = pltpu.get_barrier_semaphore()
    for x in z_peers + q_peers + c_peers:
        pl.semaphore_signal(barrier, inc=1, device_id=x, device_id_type=MESH)
    for x in loads:
        x.wait()

    def sums(t, acc):
        at = pl.multiple_of(t * 64, 64)
        v = jnp.broadcast_to(v_ref[pl.ds(t, 1), :], (128, 64)).T
        across = jnp.zeros((64, 128), F32)
        out = []
        for b in range(4):
            block = a_ref[b, pl.ds(at, 64), :]
            across = across + block * w_ref[b : b + 1, :]
            out.append(acc[b] + (block * v).reshape(8, 8, 128).sum(0))
        r_ref[pl.ds(t, 1), 0:64] = jnp.sum(across.T, axis=0, keepdims=True)
        return tuple(out)

    r_ref[...] = jnp.zeros((32, 128), F32)
    acc = lax.fori_loop(0, 32, sums, tuple(jnp.zeros((8, 128), F32) for _ in range(4)))
    for b in range(4):
        c_ref[b : b + 1, :] = jnp.sum(acc[b], axis=0, keepdims=True)
    c_ref[4:8, :] = jnp.zeros((4, 128), F32)

    @pl.when(is_root)
    def _():
        p_ref[...] = a_ref[0]

    pl.semaphore_wait(barrier, 17)

    @pl.when(heads)
    def _():
        mine = pl.ds(pl.multiple_of(col * 64, 64), 64)
        t_ref[:, mine, :] = a_ref[:, 0:64, :]

    def t_copy(part, i, src):
        blocks = pl.ds(0, 1) if part == 0 else pl.ds(1, 3)
        mine = pl.ds(pl.multiple_of(src * 64, 64), 64)
        return pltpu.make_async_remote_copy(
            t_ref.at[blocks, mine, :], t_ref.at[blocks, mine, :],
            t_send.at[part * 7 + i], t_recv.at[part * 2 + src],
            device_id=c_peers[i], device_id_type=MESH,
        )

    @pl.when(heads)
    def _():
        for i in range(7):
            t_copy(0, i, col).start()

    cz_ref[pl.ds(col, 1)] = c_ref[...][None]

    def c_copy(i):
        return pltpu.make_async_remote_copy(
            cz_ref.at[col], cz_ref.at[col], c_send.at[i], c_recv.at[i],
            device_id=c_peers[i], device_id_type=MESH,
        )

    for i in range(7):
        c_copy(i).start()

    def rq_copy(i):
        to = lax.rem(q + i + 1, 4)
        return pltpu.make_async_remote_copy(
            r_ref.at[pl.ds(pl.multiple_of(to * 8, 8), 8)], rq_ref.at[i],
            rq_send.at[i], rq_recv.at[i],
            device_id=q_peers[i], device_id_type=MESH,
        )

    for i in range(3):
        rq_copy(i).start()

    def piece(n, k):
        return pl.ds(pl.multiple_of(n * (CH * 64) + k * 64, 64), 64)

    def p_copy(n, k, send, recv, to):
        return pltpu.make_async_remote_copy(
            p_ref.at[piece(n, k)], p_ref.at[piece(n, k)],
            send.at[k], recv.at[k], device_id=to, device_id_type=MESH,
        )

    up_side = z < 4
    has_dn = jnp.logical_and(z != 4, z != 5)
    dn_to = at_row(jnp.where(up_side, z + 1, jnp.where(has_dn, z - 1, z + 1)) * 4 + q)
    dn2_to = at_row(7 * 4 + q)
    at_zero = z == 0
    to_sib = jnp.logical_not(jnp.logical_and(at_zero, q == 1))
    to_opp = jnp.logical_not(jnp.logical_and(at_zero, q == 2))
    sib_n = q + 1 - 2 * lax.rem(q, 2)
    opp_n = lax.rem(q + 2, 4)

    def pass_own(k):
        @pl.when(has_dn)
        def _():
            p_copy(q, k, dn_send, own_recv, dn_to).start()

        @pl.when(at_zero)
        def _():
            p_copy(q, k, dn2_send, own_recv, dn2_to).start()

        @pl.when(to_opp)
        def _():
            p_copy(q, k, y_send, y_recv, opp).start()

        @pl.when(to_sib)
        def _():
            p_copy(q, k, sib_send, sib_recv, sib).start()

    def pass_opp(k):
        @pl.when(to_sib)
        def _():
            p_copy(opp_n, k, rel_send, rel_recv, sib).start()

    def root_copy(n, k):
        return pltpu.make_async_remote_copy(
            p_ref.at[piece(n, k)], p_ref.at[piece(n, k)],
            root_send.at[(n - 1) * CH + k], own_recv.at[k],
            device_id=at_row(n), device_id_type=MESH,
        )

    @pl.when(is_root)
    def _():
        def body(k, _):
            for n in (2, 3, 1):
                root_copy(n, k).start()
            pass_own(k)
            pass_opp(k)
            return 0

        lax.fori_loop(0, CH, body, 0)

    @pl.when(heads)
    def _():
        for i in range(7):
            t_copy(1, i, col).start()

    for i in range(3):
        rq_copy(i).wait()
    quarter = pl.ds(pl.multiple_of(q * 8, 8), 8)
    total = r_ref[quarter, :]
    by_source = [rq_ref[i] for i in range(3)]
    total = total + by_source[0] + by_source[1] + by_source[2]
    rz_ref[pl.ds(z, 1)] = total[None]

    def rz_copy(i):
        return pltpu.make_async_remote_copy(
            rz_ref.at[z], rz_ref.at[z], rz_send.at[i], rz_recv.at[i],
            device_id=z_peers[i], device_id_type=MESH,
        )

    def rz_arrival(i):
        return pltpu.make_async_remote_copy(
            rz_ref.at[z], rz_ref.at[lax.rem(z + NZ - 1 - i, NZ)], rz_send.at[i], rz_recv.at[i],
            device_id=z_peers[i], device_id_type=MESH,
        )

    for i in range(7):
        rz_copy(i).start()

    def take_own(k, _):
        p_copy(q, k, dn_send, own_recv, dn_to).wait_recv()
        pass_own(k)
        return 0

    def take_opp(k, _):
        p_copy(opp_n, k, y_send, y_recv, opp).wait_recv()
        pass_opp(k)
        return 0

    not_root = jnp.logical_not(is_root)

    @pl.when(not_root)
    def _():
        lax.fori_loop(0, 4, take_own, 0)

    @pl.when(is_root)
    def _():
        for s in range(2):
            @pl.when(col != s)
            def _():
                t_copy(0, 0, s).wait_recv()
        eliminate(t_ref.at[0], inv_ref.at[pl.ds(0, 128)], rows_ref, low_ref)

    def rg_copy(i):
        return pltpu.make_async_remote_copy(
            rs_ref.at[quarter], rs_ref.at[quarter], rg_send.at[i], rg_recv.at[i],
            device_id=q_peers[i], device_id_type=MESH,
        )

    def rg_arrival(i):
        theirs = pl.ds(pl.multiple_of(lax.rem(q + 3 - i, 4) * 8, 8), 8)
        return pltpu.make_async_remote_copy(
            rs_ref.at[theirs], rs_ref.at[theirs], rg_send.at[i], rg_recv.at[i],
            device_id=q_peers[i], device_id_type=MESH,
        )

    for i in range(7):
        c_copy(i).wait_recv()
    over = cz_ref[0]
    for i in range(1, 8):
        over = over + cz_ref[i]
    c_ref[...] = over

    def i_copy(i, to):
        return pltpu.make_async_remote_copy(
            inv_ref, inv_ref, i_send.at[i], i_recv.at[0], device_id=to, device_id_type=MESH
        )

    def l_copy(i, to):
        return pltpu.make_async_remote_copy(
            rows_ref, rows_ref, l_send.at[i], l_recv.at[0], device_id=to, device_id_type=MESH
        )

    def inv_to(i, to):
        i_copy(i, to).start()

        @pl.when(heads)
        def _():
            l_copy(i, to).start()

    def inv_wait(i, to):
        i_copy(i, to).wait_send()

        @pl.when(heads)
        def _():
            l_copy(i, to).wait_send()

    @pl.when(is_root)
    def _():
        inv_ref[128:136, :] = over
        for i in (2, 3, 1, 4, 0, 5, 6):
            inv_to(i, z_peers[i])
        inv_to(7, opp)
        inv_to(8, sib)

    for i in range(7):
        rz_arrival(i).wait_recv()
    whole = rz_ref[0]
    for i in range(1, 8):
        whole = whole + rz_ref[i]
    rs_ref[quarter, :] = whole
    for i in range(3):
        rg_copy(i).start()

    @pl.when(not_root)
    def _():
        lax.fori_loop(4, CH, take_own, 0)
        lax.fori_loop(0, CH, take_opp, 0)

    for i in range(3):
        rg_arrival(i).wait_recv()

    def rk_copy(i):
        return pltpu.make_async_remote_copy(
            rs_ref.at[pl.ds(0, 8)], rk_ref.at[col], rk_send.at[i], rk_recv.at[col],
            device_id=c_peers[i], device_id_type=MESH,
        )

    @pl.when(heads)
    def _():
        rk_ref[pl.ds(col, 1)] = rs_ref[0:8, :][None]
        for i in range(7):
            rk_copy(i).start()

    @pl.when(not_root)
    def _():
        i_copy(0, sib).wait_recv()

        @pl.when(heads)
        def _():
            l_copy(0, sib).wait_recv()

        @pl.when(jnp.logical_and(q == 0, z > 0))
        def _():
            inv_to(7, opp)

        @pl.when(jnp.logical_or(q == 2, jnp.logical_and(q == 0, z > 0)))
        def _():
            inv_to(8, sib)

    for s in range(2):
        @pl.when(col != s)
        def _():
            @pl.when(not_root)
            def _():
                t_copy(0, 0, s).wait_recv()

            t_copy(1, 0, s).wait_recv()
            pltpu.make_async_remote_copy(
                rs_ref.at[pl.ds(0, 8)], rk_ref.at[s], rk_send.at[0], rk_recv.at[s],
                device_id=c_peers[0], device_id_type=MESH,
            ).wait_recv()

    @pl.when(not_root)
    def _():
        def body(k, _):
            p_copy(sib_n, k, sib_send, sib_recv, sib).wait_recv()
            p_copy(lax.rem(sib_n + 2, 4), k, rel_send, rel_recv, sib).wait_recv()
            return 0

        lax.fori_loop(0, CH, body, 0)

    r_ref[...] = rs_ref[...]

    @pl.when(heads)
    def _():
        for i in range(7):
            t_copy(0, i, col).wait_send()
            t_copy(1, i, col).wait_send()
            rk_copy(i).wait_send()

    for i in range(7):
        c_copy(i).wait_send()
        rz_copy(i).wait_send()
    for i in range(3):
        rg_copy(i).wait_send()

    def sent(k, _):
        @pl.when(has_dn)
        def _():
            p_copy(q, k, dn_send, own_recv, dn_to).wait_send()

        @pl.when(at_zero)
        def _():
            p_copy(q, k, dn2_send, own_recv, dn2_to).wait_send()

        @pl.when(to_opp)
        def _():
            p_copy(q, k, y_send, y_recv, opp).wait_send()

        @pl.when(to_sib)
        def _():
            p_copy(q, k, sib_send, sib_recv, sib).wait_send()
            p_copy(opp_n, k, rel_send, rel_recv, sib).wait_send()

        @pl.when(is_root)
        def _():
            for n in (1, 2, 3):
                root_copy(n, k).wait_send()

        return 0

    lax.fori_loop(0, CH, sent, 0)

    @pl.when(is_root)
    def _():
        for i in range(7):
            inv_wait(i, z_peers[i])

    @pl.when(q == 0)
    def _():
        inv_wait(7, opp)

    @pl.when(jnp.logical_or(q == 0, q == 2))
    def _():
        inv_wait(8, sib)


def dot(a, b):
    return jnp.dot(a, b, precision=highest, preferred_element_type=F32)


def dot_t(a, b):
    return lax.dot_general(
        a, b, (((1,), (1,)), ((), ())), precision=highest, preferred_element_type=F32
    )


def update(
    a_ref, p_ref, t_ref, inv_ref, rows_ref, low_ref, r_ref, rk_ref, c_ref,
    o_ref, ro_ref, co_ref, xx_ref, xl_ref, xr_ref,
):
    step = pl.program_id(0)
    me = lax.axis_index("row")
    col = lax.axis_index("col")
    keep = jnp.where(me == 0, 0.0, 1.0)
    rows = a_ref.shape[0] // 4

    @pl.when(step == 0)
    def _():
        inv = inv_ref[0:128, :]
        crossing = inv_ref[128:129, :]
        for b in range(4):
            x = dot(inv, t_ref[b])
            if b == 0:
                i0 = lax.broadcasted_iota(jnp.int32, (128, 128), 0)
                i1 = lax.broadcasted_iota(jnp.int32, (128, 128), 1)
                low = jnp.where(i0 > i1, low_ref[...], jnp.where(i0 == i1, 1.0, 0.0))
                x = jnp.where(me == 0, -dot(inv, low), x)
            hi = x.astype(BF16)
            at = slice(128 * b, 128 * b + 128)
            xx_ref[0:128, at] = hi
            xx_ref[128:256, at] = hi
            xl_ref[:, at] = (x - hi.astype(F32)).astype(BF16)
            c = c_ref[b : b + 1, :]
            if b == 0:
                c = jnp.where(me == 0, 0.0, c)
            co_ref[b : b + 1, :] = c - dot(jnp.broadcast_to(crossing, (8, 128)), x)[0:1, :]
        rk = jnp.concatenate([rk_ref[0, :, 0:64], rk_ref[1, :, 0:64]], axis=1)
        xr_ref[...] = dot_t(jnp.broadcast_to(rk[0:1, :], (8, 128)), inv)

    p = p_ref[...]
    hi = p.astype(BF16)
    lo = (p - hi.astype(F32)).astype(BF16)
    both = jnp.concatenate([hi, lo], axis=1)
    d = jnp.dot(both, xx_ref[...], preferred_element_type=F32)
    d = d + jnp.dot(hi, xl_ref[...], preferred_element_type=F32)
    for b in range(4):
        a = a_ref[pl.ds(b, rows, 4), :]
        if b == 0:
            a = jnp.where(me == 0, 0.0, a)
        o_ref[pl.ds(b, rows, 4), :] = a - d[:, 128 * b : 128 * b + 128]
    e = dot_t(xr_ref[...], p)
    for t in range(rows // 64):
        at = step * (rows // 64) + t
        ro_ref[pl.ds(at, 1), :] = r_ref[pl.ds(at, 1), 0:64] - e[0:1, 64 * t : 64 * t + 64]

    @pl.when(jnp.logical_and(step == 0, col < 2))
    def _():
        at = pl.ds(pl.multiple_of(jnp.minimum(col, 1) * 64, 64), 64)
        i0 = lax.broadcasted_iota(jnp.int32, (64, 128), 0) + col * 64
        i1 = lax.broadcasted_iota(jnp.int32, (64, 128), 1)
        kept = rows_ref[at, :]
        lin = jnp.where(i0 > i1, kept, jnp.where(i0 == i1, 1.0, 0.0))
        for b in range(4):
            u = dot(lin, t_ref[b])
            if b == 0:
                u = jnp.where(me == 0, jnp.where(i0 > i1, low_ref[at, :], kept), u)
            o_ref[pl.ds(b, 64, 4), :] = u
        rk = jnp.concatenate([rk_ref[0, :, 0:64], rk_ref[1, :, 0:64]], axis=1)
        ro_ref[0:1, :] = dot_t(jnp.broadcast_to(rk[0:1, :], (8, 128)), lin)[0:1, :]


def per_device(matrix, column_weight, row_weight):
    n_rows = matrix.shape[0] * matrix.shape[2]
    dma = pltpu.SemaphoreType.DMA
    shapes = [
        (n_rows, 128), (4, 128, 128), (136, 128), (128, 128), (128, 128),
        (32, 128), (2, 8, 128), (8, 128),
    ]
    vmem = pl.BlockSpec(memory_space=pltpu.VMEM)
    got = pl.pallas_call(
        exchange,
        out_shape=[jax.ShapeDtypeStruct(s, F32) for s in shapes],
        in_specs=[pl.BlockSpec(memory_space=pltpu.HBM)] * 3,
        out_specs=[vmem] * len(shapes),
        scratch_shapes=[
            pltpu.VMEM((4, n_rows, 128), F32),
            pltpu.VMEM((4, 128), F32),
            pltpu.VMEM((32, 64), F32),
            pltpu.VMEM((3, 8, 128), F32),
            pltpu.VMEM((8, 8, 128), F32),
            pltpu.VMEM((32, 128), F32),
            pltpu.VMEM((8, 8, 128), F32),
            dma((6,)), dma((14,)), dma((4,)),
            dma((CH,)), dma((CH,)), dma((CH,)), dma((CH,)),
            dma((CH,)), dma((CH,)), dma((CH,)), dma((CH,)), dma((CH,)), dma((3 * CH,)),
            dma((3,)), dma((3,)), dma((7,)), dma((7,)), dma((3,)), dma((3,)),
            dma((7,)), dma((2,)), dma((7,)), dma((7,)), dma((9,)), dma((1,)),
            dma((9,)), dma((1,)),
        ],
        compiler_params=pltpu.CompilerParams(
            collective_id=0, has_side_effects=True, vmem_limit_bytes=24 << 20
        ),
        name="exchange",
    )(
        matrix.reshape(n_rows, 4, 128),
        column_weight.reshape(4, 128),
        row_weight.reshape(32, 64),
    )
    rows = n_rows // STEPS
    whole = lambda s: pl.BlockSpec(s, lambda i: (0,) * len(s))
    out, r, c = pl.pallas_call(
        update,
        grid=(STEPS,),
        out_shape=[
            jax.ShapeDtypeStruct((n_rows * 4, 128), F32),
            jax.ShapeDtypeStruct((32, 64), F32),
            jax.ShapeDtypeStruct((4, 128), F32),
        ],
        in_specs=[
            pl.BlockSpec((rows * 4, 128), lambda i: (i, 0)),
            pl.BlockSpec((rows, 128), lambda i: (i, 0)),
        ]
        + [whole(s) for s in shapes[1:]],
        out_specs=[
            pl.BlockSpec((rows * 4, 128), lambda i: (i, 0)),
            whole((32, 64)),
            whole((4, 128)),
        ],
        scratch_shapes=[
            pltpu.VMEM((256, 512), BF16),
            pltpu.VMEM((128, 512), BF16),
            pltpu.VMEM((8, 128), F32),
        ],
        compiler_params=pltpu.CompilerParams(vmem_limit_bytes=24 << 20),
        name="update",
    )(matrix.reshape(n_rows * 4, 128), *got)
    return (
        out.reshape(matrix.shape),
        r.reshape(row_weight.shape),
        c.reshape(column_weight.shape),
    )


def solution(mesh):
    return jax.shard_map(
        per_device,
        mesh=mesh,
        in_specs=(
            P(None, "col", None, None, "row", None),
            P(None, "row", None),
            P(None, "col", None),
        ),
        out_specs=(
            P(None, "col", None, None, "row", None),
            P(None, "col", None),
            P(None, "row", None),
        ),
        check_vma=False,
    )
```

```python
import jax
import jax.numpy as jnp
from jax import lax
from jax.experimental import pallas as pl
from jax.experimental.pallas import tpu as pltpu
from jax.sharding import PartitionSpec as P

MESH = pl.DeviceIdType.MESH
highest = lax.Precision.HIGHEST
F32 = jnp.float32
BF16 = jnp.bfloat16
NZ = 8
CH = 8
STEPS = 8


def dot(a, b):
    return jnp.dot(a, b, precision=highest, preferred_element_type=F32)


def dot_t(a, b):
    return lax.dot_general(
        a, b, (((1,), (1,)), ((), ())), precision=highest, preferred_element_type=F32
    )


def eliminate(g_ref, inv_ref, rows_ref, cols_ref, diag_ref):
    lane = lax.broadcasted_iota(jnp.int32, (8, 128), 1)
    sub = lax.broadcasted_iota(jnp.int32, (8, 128), 0)
    full = (8, 128)
    vs = [g_ref[8 * j : 8 * j + 8, :] for j in range(16)]
    kept_cols = [jnp.zeros(full, F32) for _ in range(16)]
    for s in range(16):
        base = 8 * s
        inside = jnp.logical_and(lane >= base, lane < base + 8)
        v0 = vs[s]
        cs = [jnp.broadcast_to(v0[:, base + j : base + j + 1], full) for j in range(8)]
        factors = [
            [jnp.broadcast_to(vs[r][:, base + j : base + j + 1], full) for j in range(8)]
            if r != s else None
            for r in range(16)
        ]
        v = v0
        diag = jnp.zeros(full, F32)
        for i in range(8):
            here = lane == base + i
            at_i = sub == i
            under = sub > i
            recip = 1.0 / jnp.broadcast_to(cs[i][i : i + 1, :], full)
            ratio = cs[i] * recip
            down = jnp.where(under, ratio, 0.0)
            row = jnp.broadcast_to(v[i : i + 1, :], full)
            v = jnp.where(jnp.logical_and(here, under), -ratio, v - down * jnp.where(here, 0.0, row))
            diag = jnp.where(here, down, diag)
            for j in range(8):
                if j != i:
                    t = jnp.broadcast_to(cs[j][i : i + 1, :], full)
                    cs[j] = jnp.where(at_i, t * recip, cs[j] - ratio * t)
            cs[i] = jnp.where(at_i, recip, -ratio)
        rows_ref[base : base + 8, :] = v
        diag_ref[base : base + 8, :] = diag
        v0 = jnp.where(inside, jnp.where(lane - base == sub, 1.0, 0.0), v0)
        w = cs[0] * jnp.broadcast_to(v0[0:1, :], full)
        for j in range(1, 8):
            w = w + cs[j] * jnp.broadcast_to(v0[j : j + 1, :], full)
        wr = [jnp.broadcast_to(w[j : j + 1, :], full) for j in range(8)]
        order = [r % 16 for r in range(s + 1, s + 16)]
        for r in order:
            f = factors[r]
            a = f[0] * wr[0] + f[1] * wr[1]
            b = f[2] * wr[2] + f[3] * wr[3]
            c = f[4] * wr[4] + f[5] * wr[5]
            d = f[6] * wr[6] + f[7] * wr[7]
            new = jnp.where(inside, 0.0, vs[r]) - ((a + b) + (c + d))
            vs[r] = new
            if r > s:
                kept_cols[r] = jnp.where(inside, new, kept_cols[r])
        vs[s] = w
    for j in range(16):
        inv_ref[8 * j : 8 * j + 8, :] = vs[j]
        cols_ref[8 * j : 8 * j + 8, :] = kept_cols[j]


def exchange(
    a_hbm, w_hbm, v_hbm,
    p_ref, t_ref, inv_ref, rows_ref, low_ref, uin_ref, r_ref, rk_ref, c_ref,
    cols_ref, diag_ref, a_ref, w_ref, v_ref, rq_ref, rz_ref, rs_ref, cz_ref,
    load_sem, t_send, t_recv, own_recv, sib_recv, y_recv, rel_recv,
    dn_send, dn2_send, sib_send, y_send, rel_send, root_send,
    rq_send, rq_recv, rz_send, rz_recv, rg_send, rg_recv, rk_send, rk_recv,
    c_send, c_recv, i_send, i_recv, l_send, l_recv,
):
    me = lax.axis_index("row")
    col = lax.axis_index("col")
    z = me // 4
    q = lax.rem(me, 4)
    is_root = me == 0
    heads = col < 2

    def at_row(r):
        return dict(row=r, col=col)

    z_peers = [at_row(lax.rem(z + d, NZ) * 4 + q) for d in range(1, NZ)]
    q_peers = [at_row(z * 4 + lax.rem(q + d, 4)) for d in range(1, 4)]
    c_peers = [dict(row=me, col=lax.rem(col + d, 8)) for d in range(1, 8)]
    sib = at_row(z * 4 + (q + 1 - 2 * lax.rem(q, 2)))
    opp = at_row(z * 4 + lax.rem(q + 2, 4))

    loads = [
        pltpu.make_async_copy(a_hbm.at[:, b, :], a_ref.at[b], load_sem.at[b])
        for b in range(4)
    ]
    loads.append(pltpu.make_async_copy(w_hbm, w_ref, load_sem.at[4]))
    loads.append(pltpu.make_async_copy(v_hbm, v_ref, load_sem.at[5]))
    for x in loads:
        x.start()
    barrier = pltpu.get_barrier_semaphore()
    for x in z_peers + q_peers + c_peers:
        pl.semaphore_signal(barrier, inc=1, device_id=x, device_id_type=MESH)
    for x in loads:
        x.wait()

    def sums(t, acc):
        at = pl.multiple_of(t * 64, 64)
        v = jnp.broadcast_to(v_ref[pl.ds(t, 1), :], (128, 64)).T
        across = jnp.zeros((64, 128), F32)
        out = []
        for b in range(4):
            block = a_ref[b, pl.ds(at, 64), :]
            across = across + block * w_ref[b : b + 1, :]
            out.append(acc[b] + (block * v).reshape(8, 8, 128).sum(0))
        r_ref[pl.ds(t, 1), 0:64] = jnp.sum(across.T, axis=0, keepdims=True)
        return tuple(out)

    r_ref[...] = jnp.zeros((32, 128), F32)
    acc = lax.fori_loop(
        0, 32, sums, tuple(jnp.zeros((8, 128), F32) for _ in range(4)), unroll=4
    )
    for b in range(4):
        c_ref[b : b + 1, :] = jnp.sum(acc[b], axis=0, keepdims=True)
    c_ref[4:8, :] = jnp.zeros((4, 128), F32)

    @pl.when(is_root)
    def _():
        p_ref[...] = a_ref[0]

    pl.semaphore_wait(barrier, 17)

    @pl.when(heads)
    def _():
        mine = pl.ds(pl.multiple_of(col * 64, 64), 64)
        t_ref[:, mine, :] = a_ref[:, 0:64, :]

    def t_copy(part, i, src):
        blocks = pl.ds(0, 1) if part == 0 else pl.ds(1, 3)
        mine = pl.ds(pl.multiple_of(src * 64, 64), 64)
        return pltpu.make_async_remote_copy(
            t_ref.at[blocks, mine, :], t_ref.at[blocks, mine, :],
            t_send.at[part * 7 + i], t_recv.at[part * 2 + src],
            device_id=c_peers[i], device_id_type=MESH,
        )

    @pl.when(heads)
    def _():
        for i in range(7):
            t_copy(0, i, col).start()

    cz_ref[pl.ds(col, 1)] = c_ref[...][None]

    def c_copy(i):
        return pltpu.make_async_remote_copy(
            cz_ref.at[col], cz_ref.at[col], c_send.at[i], c_recv.at[i],
            device_id=c_peers[i], device_id_type=MESH,
        )

    for i in range(7):
        c_copy(i).start()

    def rq_copy(i):
        to = lax.rem(q + i + 1, 4)
        return pltpu.make_async_remote_copy(
            r_ref.at[pl.ds(pl.multiple_of(to * 8, 8), 8)], rq_ref.at[i],
            rq_send.at[i], rq_recv.at[i],
            device_id=q_peers[i], device_id_type=MESH,
        )

    for i in range(3):
        rq_copy(i).start()

    def piece(n, k):
        return pl.ds(pl.multiple_of(n * (CH * 64) + k * 64, 64), 64)

    def p_copy(n, k, send, recv, to):
        return pltpu.make_async_remote_copy(
            p_ref.at[piece(n, k)], p_ref.at[piece(n, k)],
            send.at[k], recv.at[k], device_id=to, device_id_type=MESH,
        )

    up_side = z < 4
    has_dn = jnp.logical_and(z != 4, z != 5)
    dn_to = at_row(jnp.where(up_side, z + 1, jnp.where(has_dn, z - 1, z + 1)) * 4 + q)
    dn2_to = at_row(7 * 4 + q)
    at_zero = z == 0
    to_sib = jnp.logical_not(jnp.logical_and(at_zero, q == 1))
    to_opp = jnp.logical_not(jnp.logical_and(at_zero, q == 2))
    sib_n = q + 1 - 2 * lax.rem(q, 2)
    opp_n = lax.rem(q + 2, 4)

    def pass_own(k):
        @pl.when(has_dn)
        def _():
            p_copy(q, k, dn_send, own_recv, dn_to).start()

        @pl.when(at_zero)
        def _():
            p_copy(q, k, dn2_send, own_recv, dn2_to).start()

        @pl.when(to_opp)
        def _():
            p_copy(q, k, y_send, y_recv, opp).start()

        @pl.when(to_sib)
        def _():
            p_copy(q, k, sib_send, sib_recv, sib).start()

    def pass_opp(k):
        @pl.when(to_sib)
        def _():
            p_copy(opp_n, k, rel_send, rel_recv, sib).start()

    def root_copy(n, k):
        return pltpu.make_async_remote_copy(
            p_ref.at[piece(n, k)], p_ref.at[piece(n, k)],
            root_send.at[(n - 1) * CH + k], own_recv.at[k],
            device_id=at_row(n), device_id_type=MESH,
        )

    @pl.when(is_root)
    def _():
        def body(k, _):
            for n in (2, 3, 1):
                root_copy(n, k).start()
            pass_own(k)
            pass_opp(k)
            return 0

        lax.fori_loop(0, CH, body, 0)

    @pl.when(heads)
    def _():
        for i in range(7):
            t_copy(1, i, col).start()

    for i in range(3):
        rq_copy(i).wait()
    quarter = pl.ds(pl.multiple_of(q * 8, 8), 8)
    total = r_ref[quarter, :]
    by_source = [rq_ref[i] for i in range(3)]
    total = total + by_source[0] + by_source[1] + by_source[2]
    rz_ref[pl.ds(z, 1)] = total[None]

    def rz_copy(i):
        return pltpu.make_async_remote_copy(
            rz_ref.at[z], rz_ref.at[z], rz_send.at[i], rz_recv.at[i],
            device_id=z_peers[i], device_id_type=MESH,
        )

    def rz_arrival(i):
        return pltpu.make_async_remote_copy(
            rz_ref.at[z], rz_ref.at[lax.rem(z + NZ - 1 - i, NZ)], rz_send.at[i], rz_recv.at[i],
            device_id=z_peers[i], device_id_type=MESH,
        )

    for i in range(7):
        rz_copy(i).start()

    def take_own(k, _):
        p_copy(q, k, dn_send, own_recv, dn_to).wait_recv()
        pass_own(k)
        return 0

    def take_opp(k, _):
        p_copy(opp_n, k, y_send, y_recv, opp).wait_recv()
        pass_opp(k)
        return 0

    not_root = jnp.logical_not(is_root)

    @pl.when(not_root)
    def _():
        lax.fori_loop(0, 4, take_own, 0)

    @pl.when(is_root)
    def _():
        for s in range(2):
            @pl.when(col != s)
            def _():
                t_copy(0, 0, s).wait_recv()
        eliminate(t_ref.at[0], inv_ref, rows_ref, cols_ref, diag_ref)

    def rg_copy(i):
        return pltpu.make_async_remote_copy(
            rs_ref.at[quarter], rs_ref.at[quarter], rg_send.at[i], rg_recv.at[i],
            device_id=q_peers[i], device_id_type=MESH,
        )

    def rg_arrival(i):
        theirs = pl.ds(pl.multiple_of(lax.rem(q + 3 - i, 4) * 8, 8), 8)
        return pltpu.make_async_remote_copy(
            rs_ref.at[theirs], rs_ref.at[theirs], rg_send.at[i], rg_recv.at[i],
            device_id=q_peers[i], device_id_type=MESH,
        )

    for i in range(7):
        c_copy(i).wait_recv()
    over = cz_ref[0]
    for i in range(1, 8):
        over = over + cz_ref[i]
    c_ref[...] = over

    def i_copy(i, to):
        return pltpu.make_async_remote_copy(
            inv_ref, inv_ref, i_send.at[i], i_recv.at[0], device_id=to, device_id_type=MESH
        )

    def l_copy(i, to):
        return pltpu.make_async_remote_copy(
            rows_ref, rows_ref, l_send.at[i], l_recv.at[0], device_id=to, device_id_type=MESH
        )

    def inv_to(i, to):
        i_copy(i, to).start()

        @pl.when(heads)
        def _():
            l_copy(i, to).start()

    def inv_wait(i, to):
        i_copy(i, to).wait_send()

        @pl.when(heads)
        def _():
            l_copy(i, to).wait_send()

    @pl.when(is_root)
    def _():
        inv_ref[128:136, :] = over
        for i in (2, 3, 1, 4, 0, 5, 6):
            inv_to(i, z_peers[i])
        inv_to(7, opp)
        inv_to(8, sib)

    @pl.when(is_root)
    def _():
        i0 = lax.broadcasted_iota(jnp.int32, (128, 128), 0)
        i1 = lax.broadcasted_iota(jnp.int32, (128, 128), 1)
        inner = diag_ref[...] + jnp.where(i0 == i1, 1.0, 0.0)
        low = jnp.where(i0 // 8 > i1 // 8, -dot(cols_ref[...], inner), inner)
        low_ref[...] = low
        uin_ref[...] = -dot(inv_ref[0:128, :], low)

    for i in range(7):
        rz_arrival(i).wait_recv()
    whole = rz_ref[0]
    for i in range(1, 8):
        whole = whole + rz_ref[i]
    rs_ref[quarter, :] = whole
    for i in range(3):
        rg_copy(i).start()

    @pl.when(not_root)
    def _():
        lax.fori_loop(4, CH, take_own, 0)
        lax.fori_loop(0, CH, take_opp, 0)

    for i in range(3):
        rg_arrival(i).wait_recv()

    def rk_copy(i):
        return pltpu.make_async_remote_copy(
            rs_ref.at[pl.ds(0, 8)], rk_ref.at[col], rk_send.at[i], rk_recv.at[col],
            device_id=c_peers[i], device_id_type=MESH,
        )

    @pl.when(heads)
    def _():
        rk_ref[pl.ds(col, 1)] = rs_ref[0:8, :][None]
        for i in range(7):
            rk_copy(i).start()

    @pl.when(not_root)
    def _():
        i_copy(0, sib).wait_recv()

        @pl.when(heads)
        def _():
            l_copy(0, sib).wait_recv()

        @pl.when(jnp.logical_and(q == 0, z > 0))
        def _():
            inv_to(7, opp)

        @pl.when(jnp.logical_or(q == 2, jnp.logical_and(q == 0, z > 0)))
        def _():
            inv_to(8, sib)

    for s in range(2):
        @pl.when(col != s)
        def _():
            @pl.when(not_root)
            def _():
                t_copy(0, 0, s).wait_recv()

            t_copy(1, 0, s).wait_recv()
            pltpu.make_async_remote_copy(
                rs_ref.at[pl.ds(0, 8)], rk_ref.at[s], rk_send.at[0], rk_recv.at[s],
                device_id=c_peers[0], device_id_type=MESH,
            ).wait_recv()

    @pl.when(not_root)
    def _():
        def body(k, _):
            p_copy(sib_n, k, sib_send, sib_recv, sib).wait_recv()
            p_copy(lax.rem(sib_n + 2, 4), k, rel_send, rel_recv, sib).wait_recv()
            return 0

        lax.fori_loop(0, CH, body, 0)

    r_ref[...] = rs_ref[...]

    @pl.when(heads)
    def _():
        for i in range(7):
            t_copy(0, i, col).wait_send()
            t_copy(1, i, col).wait_send()
            rk_copy(i).wait_send()

    for i in range(7):
        c_copy(i).wait_send()
        rz_copy(i).wait_send()
    for i in range(3):
        rg_copy(i).wait_send()

    def sent(k, _):
        @pl.when(has_dn)
        def _():
            p_copy(q, k, dn_send, own_recv, dn_to).wait_send()

        @pl.when(at_zero)
        def _():
            p_copy(q, k, dn2_send, own_recv, dn2_to).wait_send()

        @pl.when(to_opp)
        def _():
            p_copy(q, k, y_send, y_recv, opp).wait_send()

        @pl.when(to_sib)
        def _():
            p_copy(q, k, sib_send, sib_recv, sib).wait_send()
            p_copy(opp_n, k, rel_send, rel_recv, sib).wait_send()

        @pl.when(is_root)
        def _():
            for n in (1, 2, 3):
                root_copy(n, k).wait_send()

        return 0

    lax.fori_loop(0, CH, sent, 0)

    @pl.when(is_root)
    def _():
        for i in range(7):
            inv_wait(i, z_peers[i])

    @pl.when(q == 0)
    def _():
        inv_wait(7, opp)

    @pl.when(jnp.logical_or(q == 0, q == 2))
    def _():
        inv_wait(8, sib)


def update(
    a_ref, p_ref, t_ref, inv_ref, rows_ref, low_ref, uin_ref, r_ref, rk_ref, c_ref,
    o_ref, ro_ref, co_ref, xx_ref, xl_ref, xr_ref,
):
    step = pl.program_id(0)
    me = lax.axis_index("row")
    col = lax.axis_index("col")
    keep = jnp.where(me == 0, 0.0, 1.0)
    rows = a_ref.shape[0] // 4

    @pl.when(step == 0)
    def _():
        inv = inv_ref[0:128, :]
        crossing = inv_ref[128:129, :]
        for b in range(4):
            x = dot(inv, t_ref[b])
            if b == 0:
                x = jnp.where(me == 0, uin_ref[...], x)
            hi = x.astype(BF16)
            at = slice(128 * b, 128 * b + 128)
            xx_ref[0:128, at] = hi
            xx_ref[128:256, at] = hi
            xl_ref[:, at] = (x - hi.astype(F32)).astype(BF16)
            c = c_ref[b : b + 1, :]
            if b == 0:
                c = jnp.where(me == 0, 0.0, c)
            co_ref[b : b + 1, :] = c - dot(jnp.broadcast_to(crossing, (8, 128)), x)[0:1, :]
        rk = jnp.concatenate([rk_ref[0, :, 0:64], rk_ref[1, :, 0:64]], axis=1)
        xr_ref[...] = dot_t(jnp.broadcast_to(rk[0:1, :], (8, 128)), inv)

    p = p_ref[...]
    hi = p.astype(BF16)
    lo = (p - hi.astype(F32)).astype(BF16)
    both = jnp.concatenate([hi, lo], axis=1)
    d = jnp.dot(both, xx_ref[...], preferred_element_type=F32)
    d = d + jnp.dot(hi, xl_ref[...], preferred_element_type=F32)
    for b in range(4):
        a = a_ref[pl.ds(b, rows, 4), :]
        if b == 0:
            a = jnp.where(me == 0, 0.0, a)
        o_ref[pl.ds(b, rows, 4), :] = a - d[:, 128 * b : 128 * b + 128]
    e = dot_t(xr_ref[...], p)
    for t in range(rows // 64):
        at = step * (rows // 64) + t
        ro_ref[pl.ds(at, 1), :] = r_ref[pl.ds(at, 1), 0:64] - e[0:1, 64 * t : 64 * t + 64]

    @pl.when(jnp.logical_and(step == 0, col < 2))
    def _():
        at = pl.ds(pl.multiple_of(jnp.minimum(col, 1) * 64, 64), 64)
        i0 = lax.broadcasted_iota(jnp.int32, (64, 128), 0) + col * 64
        i1 = lax.broadcasted_iota(jnp.int32, (64, 128), 1)
        kept = rows_ref[at, :]
        lin = jnp.where(i0 > i1, kept, jnp.where(i0 == i1, 1.0, 0.0))
        for b in range(4):
            u = dot(lin, t_ref[b])
            if b == 0:
                u = jnp.where(me == 0, jnp.where(i0 > i1, low_ref[at, :], kept), u)
            o_ref[pl.ds(b, 64, 4), :] = u
        rk = jnp.concatenate([rk_ref[0, :, 0:64], rk_ref[1, :, 0:64]], axis=1)
        ro_ref[0:1, :] = dot_t(jnp.broadcast_to(rk[0:1, :], (8, 128)), lin)[0:1, :]


def in_hbm(x):
    return pltpu.with_memory_space_constraint(x, pltpu.HBM)


def per_device(matrix, column_weight, row_weight):
    n_rows = matrix.shape[0] * matrix.shape[2]
    dma = pltpu.SemaphoreType.DMA
    shapes = [
        (n_rows, 128), (4, 128, 128), (136, 128), (128, 128), (128, 128), (128, 128),
        (32, 128), (2, 8, 128), (8, 128),
    ]
    vmem = pl.BlockSpec(memory_space=pltpu.VMEM)
    got = pl.pallas_call(
        exchange,
        out_shape=[jax.ShapeDtypeStruct(s, F32) for s in shapes],
        in_specs=[pl.BlockSpec(memory_space=pltpu.HBM)] * 3,
        out_specs=[vmem] * len(shapes),
        scratch_shapes=[
            pltpu.VMEM((128, 128), F32),
            pltpu.VMEM((128, 128), F32),
            pltpu.VMEM((4, n_rows, 128), F32),
            pltpu.VMEM((4, 128), F32),
            pltpu.VMEM((32, 64), F32),
            pltpu.VMEM((3, 8, 128), F32),
            pltpu.VMEM((8, 8, 128), F32),
            pltpu.VMEM((32, 128), F32),
            pltpu.VMEM((8, 8, 128), F32),
            dma((6,)), dma((14,)), dma((4,)),
            dma((CH,)), dma((CH,)), dma((CH,)), dma((CH,)),
            dma((CH,)), dma((CH,)), dma((CH,)), dma((CH,)), dma((CH,)), dma((3 * CH,)),
            dma((3,)), dma((3,)), dma((7,)), dma((7,)), dma((3,)), dma((3,)),
            dma((7,)), dma((2,)), dma((7,)), dma((7,)), dma((9,)), dma((1,)),
            dma((9,)), dma((1,)),
        ],
        compiler_params=pltpu.CompilerParams(
            collective_id=0, has_side_effects=True, vmem_limit_bytes=24 << 20
        ),
        name="exchange",
    )(
        in_hbm(matrix.reshape(n_rows, 4, 128)),
        in_hbm(column_weight.reshape(4, 128)),
        in_hbm(row_weight.reshape(32, 64)),
    )
    rows = n_rows // STEPS
    whole = lambda s: pl.BlockSpec(s, lambda i: (0,) * len(s))
    out, r, c = pl.pallas_call(
        update,
        grid=(STEPS,),
        out_shape=[
            jax.ShapeDtypeStruct((n_rows * 4, 128), F32),
            jax.ShapeDtypeStruct((32, 64), F32),
            jax.ShapeDtypeStruct((4, 128), F32),
        ],
        in_specs=[
            pl.BlockSpec((rows * 4, 128), lambda i: (i, 0)),
            pl.BlockSpec((rows, 128), lambda i: (i, 0)),
        ]
        + [whole(s) for s in shapes[1:]],
        out_specs=[
            pl.BlockSpec((rows * 4, 128), lambda i: (i, 0)),
            whole((32, 64)),
            whole((4, 128)),
        ],
        scratch_shapes=[
            pltpu.VMEM((256, 512), BF16),
            pltpu.VMEM((128, 512), BF16),
            pltpu.VMEM((8, 128), F32),
        ],
        compiler_params=pltpu.CompilerParams(vmem_limit_bytes=24 << 20),
        name="update",
    )(matrix.reshape(n_rows * 4, 128), *got)
    return (
        out.reshape(matrix.shape),
        r.reshape(row_weight.shape),
        c.reshape(column_weight.shape),
    )


def solution(mesh):
    return jax.shard_map(
        per_device,
        mesh=mesh,
        in_specs=(
            P(None, "col", None, None, "row", None),
            P(None, "row", None),
            P(None, "col", None),
        ),
        out_specs=(
            P(None, "col", None, None, "row", None),
            P(None, "col", None),
            P(None, "row", None),
        ),
        check_vma=False,
    )
```

```python
import jax
import jax.numpy as jnp
from jax import lax
from jax.experimental import pallas as pl
from jax.experimental.pallas import tpu as pltpu
from jax.sharding import PartitionSpec as P

MESH = pl.DeviceIdType.MESH
highest = lax.Precision.HIGHEST
F32 = jnp.float32
BF16 = jnp.bfloat16
NZ = 8
CH = 8
STEPS = 8


def dot(a, b):
    return jnp.dot(a, b, precision=highest, preferred_element_type=F32)


def dot_t(a, b):
    return lax.dot_general(
        a, b, (((1,), (1,)), ((), ())), precision=highest, preferred_element_type=F32
    )


def eliminate(g_ref, inv_ref, rows_ref, cols_ref, diag_ref):
    lane = lax.broadcasted_iota(jnp.int32, (8, 128), 1)
    sub = lax.broadcasted_iota(jnp.int32, (8, 128), 0)
    full = (8, 128)
    vs = [g_ref[8 * j : 8 * j + 8, :] for j in range(16)]
    kept_cols = [jnp.zeros(full, F32) for _ in range(16)]
    for s in range(16):
        base = 8 * s
        inside = jnp.logical_and(lane >= base, lane < base + 8)
        v0 = vs[s]
        cs = [jnp.broadcast_to(v0[:, base + j : base + j + 1], full) for j in range(8)]
        factors = [
            [jnp.broadcast_to(vs[r][:, base + j : base + j + 1], full) for j in range(8)]
            if r != s else None
            for r in range(16)
        ]
        v = v0
        diag = jnp.zeros(full, F32)
        for i in range(8):
            here = lane == base + i
            at_i = sub == i
            under = sub > i
            recip = 1.0 / jnp.broadcast_to(cs[i][i : i + 1, :], full)
            ratio = cs[i] * recip
            down = jnp.where(under, ratio, 0.0)
            row = jnp.broadcast_to(v[i : i + 1, :], full)
            v = jnp.where(jnp.logical_and(here, under), -ratio, v - down * jnp.where(here, 0.0, row))
            diag = jnp.where(here, down, diag)
            for j in range(8):
                if j != i:
                    t = jnp.broadcast_to(cs[j][i : i + 1, :], full)
                    cs[j] = jnp.where(at_i, t * recip, cs[j] - ratio * t)
            cs[i] = jnp.where(at_i, recip, -ratio)
        rows_ref[base : base + 8, :] = v
        diag_ref[base : base + 8, :] = diag
        v0 = jnp.where(inside, jnp.where(lane - base == sub, 1.0, 0.0), v0)
        w = cs[0] * jnp.broadcast_to(v0[0:1, :], full)
        for j in range(1, 8):
            w = w + cs[j] * jnp.broadcast_to(v0[j : j + 1, :], full)
        wr = [jnp.broadcast_to(w[j : j + 1, :], full) for j in range(8)]
        order = [r % 16 for r in range(s + 1, s + 16)]
        for r in order:
            f = factors[r]
            a = f[0] * wr[0] + f[1] * wr[1]
            b = f[2] * wr[2] + f[3] * wr[3]
            c = f[4] * wr[4] + f[5] * wr[5]
            d = f[6] * wr[6] + f[7] * wr[7]
            new = jnp.where(inside, 0.0, vs[r]) - ((a + b) + (c + d))
            vs[r] = new
            if r > s:
                kept_cols[r] = jnp.where(inside, new, kept_cols[r])
        vs[s] = w
    for j in range(16):
        inv_ref[8 * j : 8 * j + 8, :] = vs[j]
        cols_ref[8 * j : 8 * j + 8, :] = kept_cols[j]


def exchange(
    a_hbm, w_hbm, v_hbm,
    p_ref, xx_ref, xl_ref, xr_ref, u_ref, r_ref, c_ref,
    t_ref, inv_ref, rows_ref, low_ref, rk_ref,
    cols_ref, diag_ref, a_ref, w_ref, v_ref, rq_ref, rz_ref, rs_ref, cz_ref,
    load_sem, t_send, t_recv, own_recv, sib_recv, y_recv, rel_recv,
    dn_send, dn2_send, sib_send, y_send, rel_send, root_send,
    rq_send, rq_recv, rz_send, rz_recv, rg_send, rg_recv, rk_send, rk_recv,
    c_send, c_recv, i_send, i_recv, l_send, l_recv,
    dn_ready, dn2_ready, z_ready, z_go,
):
    me = lax.axis_index("row")
    col = lax.axis_index("col")
    z = me // 4
    q = lax.rem(me, 4)
    is_root = me == 0
    not_root = jnp.logical_not(is_root)
    heads = col < 2
    at_zero = z == 0
    off_zero = z > 0

    def at_row(r):
        return dict(row=r, col=col)

    z_peers = [at_row(lax.rem(z + d, NZ) * 4 + q) for d in range(1, NZ)]
    q_peers = [at_row(z * 4 + lax.rem(q + d, 4)) for d in range(1, 4)]
    c_peers = [dict(row=me, col=lax.rem(col + d, 8)) for d in range(1, 8)]
    sib_n = q + 1 - 2 * lax.rem(q, 2)
    opp_n = lax.rem(q + 2, 4)
    sib = at_row(z * 4 + sib_n)
    opp = at_row(z * 4 + opp_n)
    has_dn = jnp.logical_and(z != 4, z != 5)
    dn_to = at_row(jnp.where(z < 4, z + 1, jnp.where(has_dn, z - 1, z + 1)) * 4 + q)
    dn2_to = at_row(7 * 4 + q)
    up_from = at_row(jnp.where(z > 4, lax.rem(z + 1, NZ), jnp.where(off_zero, z - 1, z + 1)) * 4 + q)

    def signal(sem, to):
        pl.semaphore_signal(sem, inc=1, device_id=to, device_id_type=MESH)

    loads = [
        pltpu.make_async_copy(a_hbm.at[:, b, :], a_ref.at[b], load_sem.at[b])
        for b in range(4)
    ]
    loads.append(pltpu.make_async_copy(w_hbm, w_ref, load_sem.at[4]))
    loads.append(pltpu.make_async_copy(v_hbm, v_ref, load_sem.at[5]))
    for x in loads:
        x.start()

    barrier = pltpu.get_barrier_semaphore()
    for x in q_peers + c_peers:
        signal(barrier, x)

    @pl.when(at_zero)
    def _():
        for x in z_peers:
            signal(barrier, x)

    @pl.when(jnp.logical_and(off_zero, has_dn))
    def _():
        signal(barrier, dn_to)

    for x in loads:
        x.wait()

    def sums(t, acc):
        at = pl.multiple_of(t * 64, 64)
        v = jnp.broadcast_to(v_ref[pl.ds(t, 1), :], (128, 64)).T
        across = jnp.zeros((64, 128), F32)
        out = []
        for b in range(4):
            block = a_ref[b, pl.ds(at, 64), :]
            across = across + block * w_ref[b : b + 1, :]
            out.append(acc[b] + (block * v).reshape(8, 8, 128).sum(0))
        r_ref[pl.ds(t, 1), 0:64] = jnp.sum(across.T, axis=0, keepdims=True)
        return tuple(out)

    r_ref[...] = jnp.zeros((32, 128), F32)
    acc = lax.fori_loop(
        0, 32, sums, tuple(jnp.zeros((8, 128), F32) for _ in range(4)), unroll=4
    )
    for b in range(4):
        c_ref[b : b + 1, :] = jnp.sum(acc[b], axis=0, keepdims=True)
    c_ref[4:8, :] = jnp.zeros((4, 128), F32)

    @pl.when(is_root)
    def _():
        p_ref[...] = a_ref[0]

    pl.semaphore_wait(
        barrier, 10 + jnp.where(at_zero, 0, 1) + jnp.where(jnp.logical_and(z > 1, z < 7), 1, 0)
    )

    @pl.when(off_zero)
    def _():
        @pl.when(z == 7)
        def _():
            signal(dn2_ready, up_from)

        @pl.when(z != 7)
        def _():
            signal(dn_ready, up_from)

        signal(z_ready, at_row(q))

    @pl.when(heads)
    def _():
        mine = pl.ds(pl.multiple_of(col * 64, 64), 64)
        t_ref[:, mine, :] = a_ref[:, 0:64, :]

    def t_copy(part, i, src):
        blocks = pl.ds(0, 1) if part == 0 else pl.ds(1, 3)
        mine = pl.ds(pl.multiple_of(src * 64, 64), 64)
        return pltpu.make_async_remote_copy(
            t_ref.at[blocks, mine, :], t_ref.at[blocks, mine, :],
            t_send.at[part * 7 + i], t_recv.at[part * 2 + src],
            device_id=c_peers[i], device_id_type=MESH,
        )

    @pl.when(heads)
    def _():
        for i in range(7):
            t_copy(0, i, col).start()

    def piece(n, k):
        return pl.ds(pl.multiple_of(n * (CH * 64) + k * 64, 64), 64)

    def p_copy(n, k, send, recv, to):
        return pltpu.make_async_remote_copy(
            p_ref.at[piece(n, k)], p_ref.at[piece(n, k)],
            send.at[k], recv.at[k], device_id=to, device_id_type=MESH,
        )

    to_sib = jnp.logical_not(jnp.logical_and(at_zero, q == 1))
    to_opp = jnp.logical_not(jnp.logical_and(at_zero, q == 2))

    def pass_dn2(k, _):
        p_copy(q, k, dn2_send, own_recv, dn2_to).start()
        return 0

    def pass_quad(k):
        @pl.when(to_opp)
        def _():
            p_copy(q, k, y_send, y_recv, opp).start()

        @pl.when(to_sib)
        def _():
            p_copy(q, k, sib_send, sib_recv, sib).start()

    def pass_opp(k):
        @pl.when(to_sib)
        def _():
            p_copy(opp_n, k, rel_send, rel_recv, sib).start()

    def root_copy(n, k):
        return pltpu.make_async_remote_copy(
            p_ref.at[piece(n, k)], p_ref.at[piece(n, k)],
            root_send.at[(n - 1) * CH + k], own_recv.at[k],
            device_id=at_row(n), device_id_type=MESH,
        )

    @pl.when(is_root)
    def _():
        def out(k, _):
            for n in (2, 3, 1):
                root_copy(n, k).start()
            return 0

        lax.fori_loop(0, CH, out, 0)

    cz_ref[pl.ds(col, 1)] = c_ref[...][None]

    def c_copy(i):
        return pltpu.make_async_remote_copy(
            cz_ref.at[col], cz_ref.at[col], c_send.at[i], c_recv.at[i],
            device_id=c_peers[i], device_id_type=MESH,
        )

    for i in range(7):
        c_copy(i).start()

    def rq_copy(i):
        to = lax.rem(q + i + 1, 4)
        return pltpu.make_async_remote_copy(
            r_ref.at[pl.ds(pl.multiple_of(to * 8, 8), 8)], rq_ref.at[i],
            rq_send.at[i], rq_recv.at[i],
            device_id=q_peers[i], device_id_type=MESH,
        )

    for i in range(3):
        rq_copy(i).start()

    @pl.when(at_zero)
    def _():
        pl.semaphore_wait(dn_ready, 1)

    @pl.when(is_root)
    def _():
        def out(k, _):
            p_copy(q, k, dn_send, own_recv, dn_to).start()
            pass_quad(k)
            pass_opp(k)
            return 0

        lax.fori_loop(0, CH, out, 0)

    @pl.when(heads)
    def _():
        for i in range(7):
            t_copy(1, i, col).start()

    quarter = pl.ds(pl.multiple_of(q * 8, 8), 8)

    def rz_copy(i):
        return pltpu.make_async_remote_copy(
            rz_ref.at[z], rz_ref.at[z], rz_send.at[i], rz_recv.at[i],
            device_id=z_peers[i], device_id_type=MESH,
        )

    def rz_arrival(i):
        return pltpu.make_async_remote_copy(
            rz_ref.at[z], rz_ref.at[lax.rem(z + NZ - 1 - i, NZ)], rz_send.at[i], rz_recv.at[i],
            device_id=z_peers[i], device_id_type=MESH,
        )

    def spread_quarter():
        for i in range(3):
            rq_copy(i).wait()
        total = r_ref[quarter, :] + rq_ref[0] + rq_ref[1] + rq_ref[2]
        rz_ref[pl.ds(z, 1)] = total[None]
        for i in range(7):
            rz_copy(i).start()

    def rg_copy(i):
        return pltpu.make_async_remote_copy(
            rs_ref.at[quarter], rs_ref.at[quarter], rg_send.at[i], rg_recv.at[i],
            device_id=q_peers[i], device_id_type=MESH,
        )

    def rg_arrival(i):
        theirs = pl.ds(pl.multiple_of(lax.rem(q + 3 - i, 4) * 8, 8), 8)
        return pltpu.make_async_remote_copy(
            rs_ref.at[theirs], rs_ref.at[theirs], rg_send.at[i], rg_recv.at[i],
            device_id=q_peers[i], device_id_type=MESH,
        )

    def gather_quarters():
        for i in range(7):
            rz_arrival(i).wait_recv()
        whole = rz_ref[0]
        for i in range(1, 8):
            whole = whole + rz_ref[i]
        rs_ref[quarter, :] = whole
        for i in range(3):
            rg_copy(i).start()

    def rk_copy(i):
        return pltpu.make_async_remote_copy(
            rs_ref.at[pl.ds(0, 8)], rk_ref.at[col], rk_send.at[i], rk_recv.at[col],
            device_id=c_peers[i], device_id_type=MESH,
        )

    def spread_pivot_checks():
        for i in range(3):
            rg_arrival(i).wait_recv()

        @pl.when(heads)
        def _():
            rk_ref[pl.ds(col, 1)] = rs_ref[0:8, :][None]
            for i in range(7):
                rk_copy(i).start()

    def take_own(k, _):
        p_copy(q, k, dn_send, own_recv, dn_to).wait_recv()

        @pl.when(has_dn)
        def _():
            p_copy(q, k, dn_send, own_recv, dn_to).start()

        pass_quad(k)
        return 0

    def take_opp(k, _):
        p_copy(opp_n, k, y_send, y_recv, opp).wait_recv()
        pass_opp(k)
        return 0

    def own(a, b):
        lax.fori_loop(a, b, take_own, 0)

    mine = pl.ds(pl.multiple_of(jnp.minimum(col, 1) * 64, 64), 64)

    def i_copy(i, to):
        return pltpu.make_async_remote_copy(
            inv_ref, inv_ref, i_send.at[i], i_recv.at[0], device_id=to, device_id_type=MESH
        )

    def l_copy(i, to):
        return pltpu.make_async_remote_copy(
            rows_ref.at[mine], rows_ref.at[mine], l_send.at[i], l_recv.at[0],
            device_id=to, device_id_type=MESH,
        )

    def inv_to(i, to):
        i_copy(i, to).start()

        @pl.when(heads)
        def _():
            l_copy(i, to).start()

    def inv_wait(i, to):
        i_copy(i, to).wait_send()

        @pl.when(heads)
        def _():
            l_copy(i, to).wait_send()

    even = lax.rem(q, 2) == 0
    over_z = jnp.logical_and(at_zero, even)
    z_order = (3, 4, 2, 5, 1, 0, 6)

    def take_inverse():
        i_copy(0, sib).wait_recv()

        @pl.when(heads)
        def _():
            l_copy(0, sib).wait_recv()

        @pl.when(over_z)
        def _():
            for i in z_order:
                inv_to(i, z_peers[i])

        @pl.when(even)
        def _():
            inv_to(8, sib)

    def sum_columns():
        for i in range(7):
            c_copy(i).wait_recv()
        over = cz_ref[0]
        for i in range(1, 8):
            over = over + cz_ref[i]
        c_ref[...] = over
        return over

    @pl.when(jnp.logical_and(at_zero, not_root))
    def _():
        own(0, 4)

    @pl.when(at_zero)
    def _():
        pl.semaphore_wait(dn2_ready, 1)
        pl.semaphore_wait(z_ready, 7)
        for x in z_peers:
            signal(z_go, x)

    @pl.when(is_root)
    def _():
        lax.fori_loop(0, CH, pass_dn2, 0)
        spread_quarter()
        for s in range(2):
            @pl.when(col != s)
            def _():
                t_copy(0, 0, s).wait_recv()
        eliminate(t_ref.at[0], inv_ref, rows_ref, cols_ref, diag_ref)
        inv_ref[128:136, :] = sum_columns()
        inv_to(7, opp)
        for i in z_order:
            inv_to(i, z_peers[i])
        inv_to(8, sib)
        gather_quarters()
        i0 = lax.broadcasted_iota(jnp.int32, (128, 128), 0)
        i1 = lax.broadcasted_iota(jnp.int32, (128, 128), 1)
        inner = diag_ref[...] + jnp.where(i0 == i1, 1.0, 0.0)
        low_ref[...] = jnp.where(i0 // 8 > i1 // 8, -dot(cols_ref[...], inner), inner)
        spread_pivot_checks()

    @pl.when(jnp.logical_and(at_zero, not_root))
    def _():
        lax.fori_loop(0, 4, pass_dn2, 0)
        spread_quarter()

        def both(k, _):
            take_own(k, 0)
            return pass_dn2(k, 0)

        lax.fori_loop(4, CH, both, 0)
        lax.fori_loop(0, CH, take_opp, 0)
        gather_quarters()
        take_inverse()
        spread_pivot_checks()

    near = jnp.logical_or(z == 1, z == 7)

    @pl.when(off_zero)
    def _():
        pl.semaphore_wait(z_go, 1)
        @pl.when(jnp.logical_and(has_dn, z != 0))
        def _():
            pl.semaphore_wait(dn_ready, 1)

        spread_quarter()

        @pl.when(near)
        def _():
            own(0, CH)
            gather_quarters()
            lax.fori_loop(0, CH, take_opp, 0)
            spread_pivot_checks()
            take_inverse()

        @pl.when(jnp.logical_not(near))
        def _():
            gather_quarters()
            own(0, 4)
            spread_pivot_checks()
            own(4, CH)
            take_inverse()
            lax.fori_loop(0, CH, take_opp, 0)

    @pl.when(not_root)
    def _():
        sum_columns()

    for s in range(2):
        @pl.when(col != s)
        def _():
            @pl.when(not_root)
            def _():
                t_copy(0, 0, s).wait_recv()

            t_copy(1, 0, s).wait_recv()
            pltpu.make_async_remote_copy(
                rs_ref.at[pl.ds(0, 8)], rk_ref.at[s], rk_send.at[0], rk_recv.at[s],
                device_id=c_peers[0], device_id_type=MESH,
            ).wait_recv()

    inv = inv_ref[0:128, :]
    crossing = inv_ref[128:136, :]
    for b in range(4):
        at = slice(128 * b, 128 * b + 128)
        c = c_ref[b : b + 1, :]
        if b == 0:
            @pl.when(is_root)
            def _():
                cols_ref[...] = -dot(inv, low_ref[...])

            @pl.when(not_root)
            def _():
                cols_ref[...] = dot(inv, t_ref[0])

            x = cols_ref[...]
            c = jnp.where(is_root, 0.0, c)
        else:
            x = dot(inv, t_ref[b])
        hi = x.astype(BF16)
        xx_ref[0:128, at] = hi
        xx_ref[128:256, at] = hi
        xl_ref[:, at] = (x - hi.astype(F32)).astype(BF16)
        c_ref[b : b + 1, :] = c - dot(crossing, x)[0:1, :]
    rk = jnp.concatenate([rk_ref[0, :, 0:64], rk_ref[1, :, 0:64]], axis=1)
    rk = jnp.broadcast_to(rk[0:1, :], (8, 128))
    xr_ref[:, 0:128] = dot_t(rk, inv)
    r_ref[...] = rs_ref[...]

    @pl.when(heads)
    def _():
        i0 = lax.broadcasted_iota(jnp.int32, (64, 128), 0) + col * 64
        i1 = lax.broadcasted_iota(jnp.int32, (64, 128), 1)
        kept = rows_ref[mine, :]
        lin = jnp.where(i0 > i1, kept, jnp.where(i0 == i1, 1.0, 0.0))
        for b in range(4):
            u_ref[b] = dot(lin, t_ref[b])

        @pl.when(is_root)
        def _():
            u_ref[0] = jnp.where(i0 > i1, low_ref[mine, :], kept)

        xr_ref[:, 128:192] = dot_t(rk, lin)

    @pl.when(not_root)
    def _():
        def body(k, _):
            p_copy(sib_n, k, sib_send, sib_recv, sib).wait_recv()
            p_copy(lax.rem(sib_n + 2, 4), k, rel_send, rel_recv, sib).wait_recv()
            return 0

        lax.fori_loop(0, CH, body, 0)

    @pl.when(heads)
    def _():
        for i in range(7):
            t_copy(0, i, col).wait_send()
            t_copy(1, i, col).wait_send()
            rk_copy(i).wait_send()

    for i in range(7):
        c_copy(i).wait_send()
        rz_copy(i).wait_send()
    for i in range(3):
        rg_copy(i).wait_send()

    def sent(k, _):
        @pl.when(has_dn)
        def _():
            p_copy(q, k, dn_send, own_recv, dn_to).wait_send()

        @pl.when(at_zero)
        def _():
            p_copy(q, k, dn2_send, own_recv, dn2_to).wait_send()

        @pl.when(to_opp)
        def _():
            p_copy(q, k, y_send, y_recv, opp).wait_send()

        @pl.when(to_sib)
        def _():
            p_copy(q, k, sib_send, sib_recv, sib).wait_send()
            p_copy(opp_n, k, rel_send, rel_recv, sib).wait_send()

        @pl.when(is_root)
        def _():
            for n in (1, 2, 3):
                root_copy(n, k).wait_send()

        return 0

    lax.fori_loop(0, CH, sent, 0)

    @pl.when(over_z)
    def _():
        for i in range(7):
            inv_wait(i, z_peers[i])

    @pl.when(is_root)
    def _():
        inv_wait(7, opp)

    @pl.when(even)
    def _():
        inv_wait(8, sib)


def update(
    a_ref, p_ref, xx_ref, xl_ref, xr_ref, u_ref, r_ref, c_ref, o_ref, ro_ref, co_ref
):
    step = pl.program_id(0)
    me = lax.axis_index("row")
    col = lax.axis_index("col")
    rows = a_ref.shape[0] // 4
    p = p_ref[...]
    hi = p.astype(BF16)
    lo = (p - hi.astype(F32)).astype(BF16)
    both = jnp.concatenate([hi, lo], axis=1)
    d = jnp.dot(both, xx_ref[...], preferred_element_type=F32)
    d = d + jnp.dot(hi, xl_ref[...], preferred_element_type=F32)
    for b in range(4):
        a = a_ref[pl.ds(b, rows, 4), :]
        if b == 0:
            a = jnp.where(me == 0, 0.0, a)
        o_ref[pl.ds(b, rows, 4), :] = a - d[:, 128 * b : 128 * b + 128]
    x = xr_ref[:, 0:128]
    xh = x.astype(BF16)
    xw = (x - xh.astype(F32)).astype(BF16)
    nt = (((1,), (1,)), ((), ()))
    pair = jnp.concatenate([xh, xw], axis=0)
    e = lax.dot_general(pair, hi, nt, preferred_element_type=F32)
    e = e[0:1, :] + e[8:9, :] + lax.dot_general(xh, lo, nt, preferred_element_type=F32)[0:1, :]
    for t in range(rows // 64):
        at = step * (rows // 64) + t
        ro_ref[pl.ds(at, 1), :] = r_ref[pl.ds(at, 1), 0:64] - e[:, 64 * t : 64 * t + 64]

    @pl.when(step == 0)
    def _():
        co_ref[...] = c_ref[0:4, :]

        @pl.when(col < 2)
        def _():
            for b in range(4):
                o_ref[pl.ds(b, 64, 4), :] = u_ref[b]
            ro_ref[0:1, :] = xr_ref[0:1, 128:192]


def in_hbm(x):
    return pltpu.with_memory_space_constraint(x, pltpu.HBM)


def per_device(matrix, column_weight, row_weight):
    n_rows = matrix.shape[0] * matrix.shape[2]
    dma = pltpu.SemaphoreType.DMA
    outs = [
        ((n_rows, 128), F32), ((256, 512), BF16), ((128, 512), BF16), ((8, 256), F32),
        ((4, 64, 128), F32), ((32, 128), F32), ((8, 128), F32),
    ]
    vmem = pl.BlockSpec(memory_space=pltpu.VMEM)
    got = pl.pallas_call(
        exchange,
        out_shape=[jax.ShapeDtypeStruct(*s) for s in outs],
        in_specs=[pl.BlockSpec(memory_space=pltpu.HBM)] * 3,
        out_specs=[vmem] * len(outs),
        scratch_shapes=[
            pltpu.VMEM((4, 128, 128), F32),
            pltpu.VMEM((136, 128), F32),
            pltpu.VMEM((128, 128), F32),
            pltpu.VMEM((128, 128), F32),
            pltpu.VMEM((2, 8, 128), F32),
            pltpu.VMEM((128, 128), F32),
            pltpu.VMEM((128, 128), F32),
            pltpu.VMEM((4, n_rows, 128), F32),
            pltpu.VMEM((4, 128), F32),
            pltpu.VMEM((32, 64), F32),
            pltpu.VMEM((3, 8, 128), F32),
            pltpu.VMEM((8, 8, 128), F32),
            pltpu.VMEM((32, 128), F32),
            pltpu.VMEM((8, 8, 128), F32),
            dma((6,)), dma((14,)), dma((4,)),
            dma((CH,)), dma((CH,)), dma((CH,)), dma((CH,)),
            dma((CH,)), dma((CH,)), dma((CH,)), dma((CH,)), dma((CH,)), dma((3 * CH,)),
            dma((3,)), dma((3,)), dma((7,)), dma((7,)), dma((3,)), dma((3,)),
            dma((7,)), dma((2,)), dma((7,)), dma((7,)), dma((9,)), dma((1,)),
            dma((9,)), dma((1,)),
        ]
        + [pltpu.SemaphoreType.REGULAR] * 4,
        compiler_params=pltpu.CompilerParams(
            collective_id=0, has_side_effects=True, vmem_limit_bytes=24 << 20
        ),
        name="exchange",
    )(
        in_hbm(matrix.reshape(n_rows, 4, 128)),
        in_hbm(column_weight.reshape(4, 128)),
        in_hbm(row_weight.reshape(32, 64)),
    )
    rows = n_rows // STEPS
    whole = lambda s: pl.BlockSpec(s, lambda i: (0,) * len(s))
    out, r, c = pl.pallas_call(
        update,
        grid=(STEPS,),
        out_shape=[
            jax.ShapeDtypeStruct((n_rows * 4, 128), F32),
            jax.ShapeDtypeStruct((32, 64), F32),
            jax.ShapeDtypeStruct((4, 128), F32),
        ],
        in_specs=[
            pl.BlockSpec((rows * 4, 128), lambda i: (i, 0)),
            pl.BlockSpec((rows, 128), lambda i: (i, 0)),
        ]
        + [whole(s) for s, _ in outs[1:]],
        out_specs=[
            pl.BlockSpec((rows * 4, 128), lambda i: (i, 0)),
            whole((32, 64)),
            whole((4, 128)),
        ],
        compiler_params=pltpu.CompilerParams(vmem_limit_bytes=24 << 20),
        name="update",
    )(matrix.reshape(n_rows * 4, 128), *got)
    return (
        out.reshape(matrix.shape),
        r.reshape(row_weight.shape),
        c.reshape(column_weight.shape),
    )


def solution(mesh):
    return jax.shard_map(
        per_device,
        mesh=mesh,
        in_specs=(
            P(None, "col", None, None, "row", None),
            P(None, "row", None),
            P(None, "col", None),
        ),
        out_specs=(
            P(None, "col", None, None, "row", None),
            P(None, "col", None),
            P(None, "row", None),
        ),
        check_vma=False,
    )
```

```python
import jax
import jax.numpy as jnp
from jax import lax
from jax.experimental import pallas as pl
from jax.experimental.pallas import tpu as pltpu
from jax.sharding import PartitionSpec as P

MESH = pl.DeviceIdType.MESH
highest = lax.Precision.HIGH
F32 = jnp.float32
BF16 = jnp.bfloat16
NZ = 8
CH = 8
PART = 512 // CH
STEPS = 2


def dot(a, b):
    return jnp.dot(a, b, precision=highest, preferred_element_type=F32)


def dot_t(a, b):
    return lax.dot_general(
        a, b, (((1,), (1,)), ((), ())), precision=highest, preferred_element_type=F32
    )


def eliminate(g_ref, inv_ref, rows_ref, cols_ref, diag_ref):
    lane = lax.broadcasted_iota(jnp.int32, (8, 128), 1)
    sub = lax.broadcasted_iota(jnp.int32, (8, 128), 0)
    full = (8, 128)
    vs = [g_ref[8 * j : 8 * j + 8, :] for j in range(16)]
    kept_cols = [jnp.zeros(full, F32) for _ in range(16)]
    for s in range(16):
        base = 8 * s
        inside = jnp.logical_and(lane >= base, lane < base + 8)
        v0 = vs[s]
        cs = [jnp.broadcast_to(v0[:, base + j : base + j + 1], full) for j in range(8)]
        factors = [
            [jnp.broadcast_to(vs[r][:, base + j : base + j + 1], full) for j in range(8)]
            if r != s else None
            for r in range(16)
        ]
        v = v0
        diag = jnp.zeros(full, F32)
        for i in range(8):
            here = lane == base + i
            at_i = sub == i
            under = sub > i
            recip = 1.0 / jnp.broadcast_to(cs[i][i : i + 1, :], full)
            ratio = cs[i] * recip
            down = jnp.where(under, ratio, 0.0)
            row = jnp.broadcast_to(v[i : i + 1, :], full)
            v = jnp.where(jnp.logical_and(here, under), -ratio, v - down * jnp.where(here, 0.0, row))
            diag = jnp.where(here, down, diag)
            for j in range(8):
                if j != i:
                    t = jnp.broadcast_to(cs[j][i : i + 1, :], full)
                    cs[j] = jnp.where(at_i, t * recip, cs[j] - ratio * t)
            cs[i] = jnp.where(at_i, recip, -ratio)
        rows_ref[base : base + 8, :] = v
        diag_ref[base : base + 8, :] = diag
        v0 = jnp.where(inside, jnp.where(lane - base == sub, 1.0, 0.0), v0)
        w = cs[0] * jnp.broadcast_to(v0[0:1, :], full)
        for j in range(1, 8):
            w = w + cs[j] * jnp.broadcast_to(v0[j : j + 1, :], full)
        wr = [jnp.broadcast_to(w[j : j + 1, :], full) for j in range(8)]
        order = [r % 16 for r in range(s + 1, s + 16)]
        for r in order:
            f = factors[r]
            a = f[0] * wr[0] + f[1] * wr[1]
            b = f[2] * wr[2] + f[3] * wr[3]
            c = f[4] * wr[4] + f[5] * wr[5]
            d = f[6] * wr[6] + f[7] * wr[7]
            new = jnp.where(inside, 0.0, vs[r]) - ((a + b) + (c + d))
            vs[r] = new
            if r > s:
                kept_cols[r] = jnp.where(inside, new, kept_cols[r])
        vs[s] = w
    for j in range(16):
        inv_ref[8 * j : 8 * j + 8, :] = vs[j]
        cols_ref[8 * j : 8 * j + 8, :] = kept_cols[j]


def exchange(
    a_hbm, w_hbm, v_hbm,
    p_ref, xx_ref, xl_ref, xr_ref, u_ref, r_ref, c_ref,
    t_ref, inv_ref, rows_ref, low_ref, rk_ref,
    cols_ref, diag_ref, a_ref, w_ref, v_ref, rq_ref, rz_ref, rs_ref, cz_ref, kq_ref, kz_ref,
    load_sem, t_send, t_recv, own_recv, sib_recv, y_recv, rel_recv,
    dn_send, dn2_send, sib_send, y_send, rel_send, root_send,
    rq_send, rq_recv, rz_send, rz_recv, rg_send, rg_recv, rk_send, rk_recv,
    c_send, c_recv, i_send, i_recv, l_send, l_recv, kq_send, kq_recv, kz_send, kz_recv,
    dn_ready, dn2_ready, z_ready, z_go,
):
    me = lax.axis_index("row")
    col = lax.axis_index("col")
    z = me // 4
    q = lax.rem(me, 4)
    is_root = me == 0
    not_root = jnp.logical_not(is_root)
    heads = col < 2
    at_zero = z == 0
    off_zero = z > 0

    def at_row(r):
        return dict(row=r, col=col)

    z_peers = [at_row(lax.rem(z + d, NZ) * 4 + q) for d in range(1, NZ)]
    q_peers = [at_row(z * 4 + lax.rem(q + d, 4)) for d in range(1, 4)]
    c_peers = [dict(row=me, col=lax.rem(col + d, 8)) for d in range(1, 8)]
    sib_n = q + 1 - 2 * lax.rem(q, 2)
    opp_n = lax.rem(q + 2, 4)
    sib = at_row(z * 4 + sib_n)
    opp = at_row(z * 4 + opp_n)
    has_dn = jnp.logical_and(z != 4, z != 5)
    dn_to = at_row(jnp.where(z < 4, z + 1, jnp.where(has_dn, z - 1, z + 1)) * 4 + q)
    dn2_to = at_row(7 * 4 + q)
    up_from = at_row(jnp.where(z > 4, lax.rem(z + 1, NZ), jnp.where(off_zero, z - 1, z + 1)) * 4 + q)

    def signal(sem, to):
        pl.semaphore_signal(sem, inc=1, device_id=to, device_id_type=MESH)

    loads = [
        pltpu.make_async_copy(a_hbm.at[:, b, :], a_ref.at[b], load_sem.at[b])
        for b in range(4)
    ]
    loads.append(pltpu.make_async_copy(w_hbm, w_ref, load_sem.at[4]))
    loads.append(pltpu.make_async_copy(v_hbm, v_ref, load_sem.at[5]))
    for x in loads:
        x.start()
    panel_load = pltpu.make_async_copy(a_hbm.at[:, 0, :], p_ref, load_sem.at[6])

    @pl.when(is_root)
    def _():
        panel_load.start()

    barrier = pltpu.get_barrier_semaphore()
    for x in q_peers + c_peers:
        signal(barrier, x)

    @pl.when(at_zero)
    def _():
        for x in z_peers:
            signal(barrier, x)

    @pl.when(jnp.logical_and(off_zero, has_dn))
    def _():
        signal(barrier, dn_to)

    pl.semaphore_wait(
        barrier, 10 + jnp.where(at_zero, 0, 1) + jnp.where(jnp.logical_and(z > 1, z < 7), 1, 0)
    )

    @pl.when(off_zero)
    def _():
        @pl.when(z == 7)
        def _():
            signal(dn2_ready, up_from)

        @pl.when(z != 7)
        def _():
            signal(dn_ready, up_from)

        signal(z_ready, at_row(q))

    for x in loads:
        x.wait()

    @pl.when(heads)
    def _():
        mine = pl.ds(pl.multiple_of(col * 64, 64), 64)
        t_ref[:, mine, :] = a_ref[:, 0:64, :]

    def t_copy(part, i, src):
        blocks = pl.ds(0, 1) if part == 0 else pl.ds(1, 3)
        mine = pl.ds(pl.multiple_of(src * 64, 64), 64)
        return pltpu.make_async_remote_copy(
            t_ref.at[blocks, mine, :], t_ref.at[blocks, mine, :],
            t_send.at[part * 7 + i], t_recv.at[part * 2 + src],
            device_id=c_peers[i], device_id_type=MESH,
        )

    @pl.when(heads)
    def _():
        for i in range(7):
            t_copy(0, i, col).start()

    def sums(t, acc):
        at = pl.multiple_of(t * 64, 64)
        v = jnp.broadcast_to(v_ref[pl.ds(t, 1), :], (128, 64)).T
        across = jnp.zeros((64, 128), F32)
        out = []
        for b in range(4):
            block = a_ref[b, pl.ds(at, 64), :]
            across = across + block * w_ref[b : b + 1, :]
            out.append(acc[b] + (block * v).reshape(8, 8, 128).sum(0))
        r_ref[pl.ds(t, 1), 0:64] = jnp.sum(across.T, axis=0, keepdims=True)
        return tuple(out)

    r_ref[...] = jnp.zeros((32, 128), F32)
    acc = lax.fori_loop(
        0, 32, sums, tuple(jnp.zeros((8, 128), F32) for _ in range(4)), unroll=4
    )
    for b in range(4):
        c_ref[b : b + 1, :] = jnp.sum(acc[b], axis=0, keepdims=True)
    c_ref[4:8, :] = jnp.zeros((4, 128), F32)

    cz_ref[pl.ds(col, 1)] = c_ref[...][None]

    def c_copy(i):
        return pltpu.make_async_remote_copy(
            cz_ref.at[col], cz_ref.at[col], c_send.at[i], c_recv.at[i],
            device_id=c_peers[i], device_id_type=MESH,
        )

    for i in range(7):
        c_copy(i).start()

    def rq_copy(i):
        to = lax.rem(q + i + 1, 4)
        return pltpu.make_async_remote_copy(
            r_ref.at[pl.ds(pl.multiple_of(to * 8, 8), 8)], rq_ref.at[i],
            rq_send.at[i], rq_recv.at[i],
            device_id=q_peers[i], device_id_type=MESH,
        )

    for i in range(3):
        rq_copy(i).start()

    kq_ref[pl.ds(q, 1)] = r_ref[0:8, :][None]

    def kq_copy(i):
        return pltpu.make_async_remote_copy(
            kq_ref.at[q], kq_ref.at[q], kq_send.at[i], kq_recv.at[i],
            device_id=q_peers[i], device_id_type=MESH,
        )

    def kz_copy(i):
        return pltpu.make_async_remote_copy(
            kz_ref.at[z], kz_ref.at[z], kz_send.at[i], kz_recv.at[i],
            device_id=z_peers[i], device_id_type=MESH,
        )

    def kq_arrival(i):
        return pltpu.make_async_remote_copy(
            kq_ref.at[q], kq_ref.at[lax.rem(q + 3 - i, 4)], kq_send.at[i], kq_recv.at[i],
            device_id=q_peers[i], device_id_type=MESH,
        )

    def kz_arrival(i):
        return pltpu.make_async_remote_copy(
            kz_ref.at[z], kz_ref.at[lax.rem(z + NZ - 1 - i, NZ)], kz_send.at[i], kz_recv.at[i],
            device_id=z_peers[i], device_id_type=MESH,
        )

    @pl.when(heads)
    def _():
        for i in range(3):
            kq_copy(i).start()

    def piece(n, k):
        return pl.ds(pl.multiple_of(n * 512 + k * PART, PART), PART)

    def p_copy(n, k, send, recv, to):
        return pltpu.make_async_remote_copy(
            p_ref.at[piece(n, k)], p_ref.at[piece(n, k)],
            send.at[k], recv.at[k], device_id=to, device_id_type=MESH,
        )

    to_sib = jnp.logical_not(jnp.logical_and(at_zero, q == 1))
    to_opp = jnp.logical_not(jnp.logical_and(at_zero, q == 2))

    def pass_dn2(k, _):
        p_copy(q, k, dn2_send, own_recv, dn2_to).start()
        return 0

    def pass_quad(k):
        @pl.when(to_opp)
        def _():
            p_copy(q, k, y_send, y_recv, opp).start()

        @pl.when(to_sib)
        def _():
            p_copy(q, k, sib_send, sib_recv, sib).start()

    def pass_opp(k):
        @pl.when(to_sib)
        def _():
            p_copy(opp_n, k, rel_send, rel_recv, sib).start()

    def root_copy(n, k):
        return pltpu.make_async_remote_copy(
            p_ref.at[piece(n, k)], p_ref.at[piece(n, k)],
            root_send.at[(n - 1) * CH + k], own_recv.at[k],
            device_id=at_row(n), device_id_type=MESH,
        )

    @pl.when(is_root)
    def _():
        panel_load.wait()

    @pl.when(at_zero)
    def _():
        pl.semaphore_wait(dn_ready, 1)

    @pl.when(is_root)
    def _():
        def out(k, _):
            root_copy(2, k).start()
            p_copy(q, k, dn_send, own_recv, dn_to).start()
            root_copy(3, k).start()
            root_copy(1, k).start()
            return 0

        lax.fori_loop(0, CH, out, 0)

    @pl.when(heads)
    def _():
        for i in range(7):
            t_copy(1, i, col).start()

    quarter = pl.ds(pl.multiple_of(q * 8, 8), 8)

    def rz_copy(i):
        return pltpu.make_async_remote_copy(
            rz_ref.at[z], rz_ref.at[z], rz_send.at[i], rz_recv.at[i],
            device_id=z_peers[i], device_id_type=MESH,
        )

    def rz_arrival(i):
        return pltpu.make_async_remote_copy(
            rz_ref.at[z], rz_ref.at[lax.rem(z + NZ - 1 - i, NZ)], rz_send.at[i], rz_recv.at[i],
            device_id=z_peers[i], device_id_type=MESH,
        )

    def spread_quarter():
        @pl.when(heads)
        def _():
            for i in range(3):
                kq_copy(i).wait_send()
                kq_arrival(i).wait_recv()
            kz_ref[pl.ds(z, 1)] = (kq_ref[0] + kq_ref[1] + kq_ref[2] + kq_ref[3])[None]
            for i in range(7):
                kz_copy(i).start()

        for i in range(3):
            rq_copy(i).wait()
        total = r_ref[quarter, :] + rq_ref[0] + rq_ref[1] + rq_ref[2]
        rz_ref[pl.ds(z, 1)] = total[None]
        for i in range(7):
            rz_copy(i).start()

    def rg_copy(i):
        return pltpu.make_async_remote_copy(
            rs_ref.at[quarter], rs_ref.at[quarter], rg_send.at[i], rg_recv.at[i],
            device_id=q_peers[i], device_id_type=MESH,
        )

    def rg_arrival(i):
        theirs = pl.ds(pl.multiple_of(lax.rem(q + 3 - i, 4) * 8, 8), 8)
        return pltpu.make_async_remote_copy(
            rs_ref.at[theirs], rs_ref.at[theirs], rg_send.at[i], rg_recv.at[i],
            device_id=q_peers[i], device_id_type=MESH,
        )

    def rk_copy(i):
        return pltpu.make_async_remote_copy(
            rk_ref.at[col], rk_ref.at[col], rk_send.at[i], rk_recv.at[col],
            device_id=c_peers[i], device_id_type=MESH,
        )

    def gather_quarters():
        @pl.when(heads)
        def _():
            for i in range(7):
                kz_arrival(i).wait_recv()
            top = kz_ref[0]
            for i in range(1, 8):
                top = top + kz_ref[i]
            rk_ref[pl.ds(col, 1)] = top[None]
            for i in range(7):
                rk_copy(i).start()

        for i in range(7):
            rz_arrival(i).wait_recv()
        whole = rz_ref[0]
        for i in range(1, 8):
            whole = whole + rz_ref[i]
        rs_ref[quarter, :] = whole
        for i in range(3):
            rg_copy(i).start()

    def take_own(k, _):
        p_copy(q, k, dn_send, own_recv, dn_to).wait_recv()

        @pl.when(has_dn)
        def _():
            p_copy(q, k, dn_send, own_recv, dn_to).start()

        pass_quad(k)
        return 0

    def take_opp(k, _):
        p_copy(opp_n, k, y_send, y_recv, opp).wait_recv()
        pass_opp(k)
        return 0

    def own(a, b):
        lax.fori_loop(a, b, take_own, 0)

    mine = pl.ds(pl.multiple_of(jnp.minimum(col, 1) * 64, 64), 64)

    def i_copy(i, to):
        return pltpu.make_async_remote_copy(
            inv_ref, inv_ref, i_send.at[i], i_recv.at[0], device_id=to, device_id_type=MESH
        )

    def l_copy(i, to):
        return pltpu.make_async_remote_copy(
            rows_ref.at[mine], rows_ref.at[mine], l_send.at[i], l_recv.at[0],
            device_id=to, device_id_type=MESH,
        )

    def inv_to(i, to):
        i_copy(i, to).start()

        @pl.when(heads)
        def _():
            l_copy(i, to).start()

    def inv_wait(i, to):
        i_copy(i, to).wait_send()

        @pl.when(heads)
        def _():
            l_copy(i, to).wait_send()

    even = lax.rem(q, 2) == 0
    over_z = jnp.logical_and(at_zero, even)
    z_order = (0, 6, 1, 5, 2, 4, 3)

    def take_inverse():
        i_copy(0, sib).wait_recv()

        @pl.when(heads)
        def _():
            l_copy(0, sib).wait_recv()

        @pl.when(over_z)
        def _():
            for i in z_order:
                inv_to(i, z_peers[i])

        @pl.when(even)
        def _():
            inv_to(8, sib)

    def sum_columns():
        for i in range(7):
            c_copy(i).wait_recv()
        over = cz_ref[0]
        for i in range(1, 8):
            over = over + cz_ref[i]
        c_ref[...] = over
        return over

    @pl.when(jnp.logical_and(at_zero, not_root))
    def _():
        own(0, 2)

    @pl.when(at_zero)
    def _():
        pl.semaphore_wait(dn2_ready, 1)
        pl.semaphore_wait(z_ready, 7)
        for x in z_peers:
            signal(z_go, x)

    @pl.when(is_root)
    def _():
        lax.fori_loop(0, CH, pass_dn2, 0)
        spread_quarter()

        def rest(k, _):
            pass_quad(k)
            pass_opp(k)
            return 0

        lax.fori_loop(0, CH, rest, 0)
        for s in range(2):
            @pl.when(col != s)
            def _():
                t_copy(0, 0, s).wait_recv()
        eliminate(t_ref.at[0], inv_ref, rows_ref, cols_ref, diag_ref)
        inv_ref[128:136, :] = sum_columns()
        inv_to(7, opp)
        for i in z_order:
            inv_to(i, z_peers[i])
        inv_to(8, sib)
        gather_quarters()
        i0 = lax.broadcasted_iota(jnp.int32, (128, 128), 0)
        i1 = lax.broadcasted_iota(jnp.int32, (128, 128), 1)
        inner = diag_ref[...] + jnp.where(i0 == i1, 1.0, 0.0)
        low_ref[...] = jnp.where(i0 // 8 > i1 // 8, -dot(cols_ref[...], inner), inner)

    @pl.when(jnp.logical_and(at_zero, not_root))
    def _():
        lax.fori_loop(0, 2, pass_dn2, 0)
        spread_quarter()

        def both(k, _):
            take_own(k, 0)
            return pass_dn2(k, 0)

        lax.fori_loop(2, CH, both, 0)
        gather_quarters()
        lax.fori_loop(0, CH, take_opp, 0)
        take_inverse()

    away = jnp.where(z <= 4, z, NZ - z)
    early = jnp.where(away <= 1, CH, jnp.where(away == 2, CH // 2, 0))
    before = jnp.where(away <= 1, CH, 0)

    @pl.when(off_zero)
    def _():
        pl.semaphore_wait(z_go, 1)
        @pl.when(jnp.logical_and(has_dn, z != 0))
        def _():
            pl.semaphore_wait(dn_ready, 1)

        spread_quarter()

        own(0, early)
        gather_quarters()
        own(early, CH)
        lax.fori_loop(0, before, take_opp, 0)
        take_inverse()
        lax.fori_loop(before, CH, take_opp, 0)

    @pl.when(not_root)
    def _():
        sum_columns()

    for s in range(2):
        @pl.when(col != s)
        def _():
            @pl.when(not_root)
            def _():
                t_copy(0, 0, s).wait_recv()

            t_copy(1, 0, s).wait_recv()
            pltpu.make_async_remote_copy(
                rk_ref.at[s], rk_ref.at[s], rk_send.at[0], rk_recv.at[s],
                device_id=c_peers[0], device_id_type=MESH,
            ).wait_recv()

    inv = inv_ref[0:128, :]
    crossing = inv_ref[128:136, :]
    for b in range(4):
        at = slice(128 * b, 128 * b + 128)
        c = c_ref[b : b + 1, :]
        if b == 0:
            @pl.when(is_root)
            def _():
                cols_ref[...] = -dot(inv, low_ref[...])

            @pl.when(not_root)
            def _():
                cols_ref[...] = dot(inv, t_ref[0])

            x = cols_ref[...]
            c = jnp.where(is_root, 0.0, c)
        else:
            x = dot(inv, t_ref[b])
        hi = x.astype(BF16)
        xx_ref[0:128, at] = hi
        xx_ref[128:256, at] = hi
        xl_ref[:, at] = (x - hi.astype(F32)).astype(BF16)
        c_ref[b : b + 1, :] = c - dot(crossing, x)[0:1, :]
    rk = jnp.concatenate([rk_ref[0, :, 0:64], rk_ref[1, :, 0:64]], axis=1)
    rk = jnp.broadcast_to(rk[0:1, :], (8, 128))
    xr_ref[:, 0:128] = dot_t(rk, inv)
    for i in range(3):
        rg_arrival(i).wait_recv()
    r_ref[...] = rs_ref[...]

    @pl.when(heads)
    def _():
        i0 = lax.broadcasted_iota(jnp.int32, (64, 128), 0) + col * 64
        i1 = lax.broadcasted_iota(jnp.int32, (64, 128), 1)
        kept = rows_ref[mine, :]
        lin = jnp.where(i0 > i1, kept, jnp.where(i0 == i1, 1.0, 0.0))
        for b in range(4):
            u_ref[b] = dot(lin, t_ref[b])

        @pl.when(is_root)
        def _():
            u_ref[0] = jnp.where(i0 > i1, low_ref[mine, :], kept)

        xr_ref[:, 128:192] = dot_t(rk, lin)

    @pl.when(not_root)
    def _():
        def body(k, _):
            p_copy(sib_n, k, sib_send, sib_recv, sib).wait_recv()
            p_copy(lax.rem(sib_n + 2, 4), k, rel_send, rel_recv, sib).wait_recv()
            return 0

        lax.fori_loop(0, CH, body, 0)

    @pl.when(heads)
    def _():
        for i in range(7):
            t_copy(0, i, col).wait_send()
            t_copy(1, i, col).wait_send()
            rk_copy(i).wait_send()
            kz_copy(i).wait_send()

    for i in range(7):
        c_copy(i).wait_send()
        rz_copy(i).wait_send()
    for i in range(3):
        rg_copy(i).wait_send()

    def sent(k, _):
        @pl.when(has_dn)
        def _():
            p_copy(q, k, dn_send, own_recv, dn_to).wait_send()

        @pl.when(at_zero)
        def _():
            p_copy(q, k, dn2_send, own_recv, dn2_to).wait_send()

        @pl.when(to_opp)
        def _():
            p_copy(q, k, y_send, y_recv, opp).wait_send()

        @pl.when(to_sib)
        def _():
            p_copy(q, k, sib_send, sib_recv, sib).wait_send()
            p_copy(opp_n, k, rel_send, rel_recv, sib).wait_send()

        @pl.when(is_root)
        def _():
            for n in (1, 2, 3):
                root_copy(n, k).wait_send()

        return 0

    lax.fori_loop(0, CH, sent, 0)

    @pl.when(over_z)
    def _():
        for i in range(7):
            inv_wait(i, z_peers[i])

    @pl.when(is_root)
    def _():
        inv_wait(7, opp)

    @pl.when(even)
    def _():
        inv_wait(8, sib)


def update(
    a_ref, p_ref, xx_ref, xl_ref, xr_ref, u_ref, r_ref, c_ref, o_ref, ro_ref, co_ref
):
    step = pl.program_id(0)
    me = lax.axis_index("row")
    col = lax.axis_index("col")
    rows = a_ref.shape[0] // 4
    p = p_ref[...]
    hi = p.astype(BF16)
    lo = (p - hi.astype(F32)).astype(BF16)
    both = jnp.concatenate([hi, lo], axis=1)
    d = jnp.dot(both, xx_ref[...], preferred_element_type=F32)
    d = d + jnp.dot(hi, xl_ref[...], preferred_element_type=F32)
    for b in range(4):
        a = a_ref[pl.ds(b, rows, 4), :]
        if b == 0:
            a = jnp.where(me == 0, 0.0, a)
        o_ref[pl.ds(b, rows, 4), :] = a - d[:, 128 * b : 128 * b + 128]
    x = xr_ref[:, 0:128]
    xh = x.astype(BF16)
    xw = (x - xh.astype(F32)).astype(BF16)
    nt = (((1,), (1,)), ((), ()))
    pair = jnp.concatenate([xh, xw], axis=0)
    e = lax.dot_general(pair, hi, nt, preferred_element_type=F32)
    e = e[0:1, :] + e[8:9, :] + lax.dot_general(xh, lo, nt, preferred_element_type=F32)[0:1, :]
    for t in range(rows // 64):
        at = step * (rows // 64) + t
        ro_ref[pl.ds(at, 1), :] = r_ref[pl.ds(at, 1), 0:64] - e[:, 64 * t : 64 * t + 64]

    @pl.when(step == 0)
    def _():
        co_ref[...] = c_ref[0:4, :]

        @pl.when(col < 2)
        def _():
            for b in range(4):
                o_ref[pl.ds(b, 64, 4), :] = u_ref[b]
            ro_ref[0:1, :] = xr_ref[0:1, 128:192]


def in_hbm(x):
    return pltpu.with_memory_space_constraint(x, pltpu.HBM)


def per_device(matrix, column_weight, row_weight):
    n_rows = matrix.shape[0] * matrix.shape[2]
    dma = pltpu.SemaphoreType.DMA
    outs = [
        ((n_rows, 128), F32), ((256, 512), BF16), ((128, 512), BF16), ((8, 256), F32),
        ((4, 64, 128), F32), ((32, 128), F32), ((8, 128), F32),
    ]
    vmem = pl.BlockSpec(memory_space=pltpu.VMEM)
    got = pl.pallas_call(
        exchange,
        out_shape=[jax.ShapeDtypeStruct(*s) for s in outs],
        in_specs=[pl.BlockSpec(memory_space=pltpu.HBM)] * 3,
        out_specs=[vmem] * len(outs),
        scratch_shapes=[
            pltpu.VMEM((4, 128, 128), F32),
            pltpu.VMEM((136, 128), F32),
            pltpu.VMEM((128, 128), F32),
            pltpu.VMEM((128, 128), F32),
            pltpu.VMEM((2, 8, 128), F32),
            pltpu.VMEM((128, 128), F32),
            pltpu.VMEM((128, 128), F32),
            pltpu.VMEM((4, n_rows, 128), F32),
            pltpu.VMEM((4, 128), F32),
            pltpu.VMEM((32, 64), F32),
            pltpu.VMEM((3, 8, 128), F32),
            pltpu.VMEM((8, 8, 128), F32),
            pltpu.VMEM((32, 128), F32),
            pltpu.VMEM((8, 8, 128), F32),
            pltpu.VMEM((4, 8, 128), F32),
            pltpu.VMEM((8, 8, 128), F32),
            dma((7,)), dma((14,)), dma((4,)),
            dma((CH,)), dma((CH,)), dma((CH,)), dma((CH,)),
            dma((CH,)), dma((CH,)), dma((CH,)), dma((CH,)), dma((CH,)), dma((3 * CH,)),
            dma((3,)), dma((3,)), dma((7,)), dma((7,)), dma((3,)), dma((3,)),
            dma((7,)), dma((2,)), dma((7,)), dma((7,)), dma((9,)), dma((1,)),
            dma((9,)), dma((1,)), dma((3,)), dma((3,)), dma((7,)), dma((7,)),
        ]
        + [pltpu.SemaphoreType.REGULAR] * 4,
        compiler_params=pltpu.CompilerParams(
            collective_id=0, has_side_effects=True, vmem_limit_bytes=24 << 20
        ),
        name="exchange",
    )(
        in_hbm(matrix.reshape(n_rows, 4, 128)),
        in_hbm(column_weight.reshape(4, 128)),
        in_hbm(row_weight.reshape(32, 64)),
    )
    rows = n_rows // STEPS
    whole = lambda s: pl.BlockSpec(s, lambda i: (0,) * len(s))
    out, r, c = pl.pallas_call(
        update,
        grid=(STEPS,),
        out_shape=[
            jax.ShapeDtypeStruct((n_rows * 4, 128), F32),
            jax.ShapeDtypeStruct((32, 64), F32),
            jax.ShapeDtypeStruct((4, 128), F32),
        ],
        in_specs=[
            pl.BlockSpec((rows * 4, 128), lambda i: (i, 0)),
            pl.BlockSpec((rows, 128), lambda i: (i, 0)),
        ]
        + [whole(s) for s, _ in outs[1:]],
        out_specs=[
            pl.BlockSpec((rows * 4, 128), lambda i: (i, 0)),
            whole((32, 64)),
            whole((4, 128)),
        ],
        compiler_params=pltpu.CompilerParams(vmem_limit_bytes=24 << 20),
        name="update",
    )(matrix.reshape(n_rows * 4, 128), *got)
    return (
        out.reshape(matrix.shape),
        r.reshape(row_weight.shape),
        c.reshape(column_weight.shape),
    )


def solution(mesh):
    return jax.shard_map(
        per_device,
        mesh=mesh,
        in_specs=(
            P(None, "col", None, None, "row", None),
            P(None, "row", None),
            P(None, "col", None),
        ),
        out_specs=(
            P(None, "col", None, None, "row", None),
            P(None, "col", None),
            P(None, "row", None),
        ),
        check_vma=False,
    )
```

```python
import jax
import jax.numpy as jnp
from jax import lax
from jax.experimental import pallas as pl
from jax.experimental.pallas import tpu as pltpu
from jax.sharding import PartitionSpec as P

MESH = pl.DeviceIdType.MESH
highest = lax.Precision.HIGH
F32 = jnp.float32
BF16 = jnp.bfloat16
NZ = 8
PART = 64
LONG = 10
SHORT = 6
HEADSTART = 4
STEPS = 2


def dot(a, b):
    return jnp.dot(a, b, precision=highest, preferred_element_type=F32)


def dot_t(a, b):
    return lax.dot_general(
        a, b, (((1,), (1,)), ((), ())), precision=highest, preferred_element_type=F32
    )


def eliminate(g_ref, inv_ref, rows_ref, cols_ref, diag_ref):
    lane = lax.broadcasted_iota(jnp.int32, (8, 128), 1)
    sub = lax.broadcasted_iota(jnp.int32, (8, 128), 0)
    full = (8, 128)
    vs = [g_ref[8 * j : 8 * j + 8, :] for j in range(16)]
    kept_cols = [jnp.zeros(full, F32) for _ in range(16)]
    for s in range(16):
        base = 8 * s
        inside = jnp.logical_and(lane >= base, lane < base + 8)
        v0 = vs[s]
        cs = [jnp.broadcast_to(v0[:, base + j : base + j + 1], full) for j in range(8)]
        factors = [
            [jnp.broadcast_to(vs[r][:, base + j : base + j + 1], full) for j in range(8)]
            if r != s else None
            for r in range(16)
        ]
        v = v0
        diag = jnp.zeros(full, F32)
        for i in range(8):
            here = lane == base + i
            at_i = sub == i
            under = sub > i
            recip = 1.0 / jnp.broadcast_to(cs[i][i : i + 1, :], full)
            ratio = cs[i] * recip
            down = jnp.where(under, ratio, 0.0)
            row = jnp.broadcast_to(v[i : i + 1, :], full)
            v = jnp.where(jnp.logical_and(here, under), -ratio, v - down * jnp.where(here, 0.0, row))
            diag = jnp.where(here, down, diag)
            for j in range(8):
                if j != i:
                    t = jnp.broadcast_to(cs[j][i : i + 1, :], full)
                    cs[j] = jnp.where(at_i, t * recip, cs[j] - ratio * t)
            cs[i] = jnp.where(at_i, recip, -ratio)
        rows_ref[base : base + 8, :] = v
        diag_ref[base : base + 8, :] = diag
        v0 = jnp.where(inside, jnp.where(lane - base == sub, 1.0, 0.0), v0)
        w = cs[0] * jnp.broadcast_to(v0[0:1, :], full)
        for j in range(1, 8):
            w = w + cs[j] * jnp.broadcast_to(v0[j : j + 1, :], full)
        wr = [jnp.broadcast_to(w[j : j + 1, :], full) for j in range(8)]
        order = [r % 16 for r in range(s + 1, s + 16)]
        for r in order:
            f = factors[r]
            a = f[0] * wr[0] + f[1] * wr[1]
            b = f[2] * wr[2] + f[3] * wr[3]
            c = f[4] * wr[4] + f[5] * wr[5]
            d = f[6] * wr[6] + f[7] * wr[7]
            new = jnp.where(inside, 0.0, vs[r]) - ((a + b) + (c + d))
            vs[r] = new
            if r > s:
                kept_cols[r] = jnp.where(inside, new, kept_cols[r])
        vs[s] = w
    for j in range(16):
        inv_ref[8 * j : 8 * j + 8, :] = vs[j]
        cols_ref[8 * j : 8 * j + 8, :] = kept_cols[j]


def exchange(
    a_hbm, w_hbm, v_hbm,
    p_ref, xx_ref, xl_ref, xr_ref, u_ref, r_ref, c_ref,
    t_ref, inv_ref, rows_ref, low_ref, rk_ref,
    cols_ref, diag_ref, a_ref, w_ref, v_ref, rq_ref, rz_ref, rs_ref, cz_ref, kq_ref, kz_ref,
    load_sem, t_send, t_recv, own_recv, sib_recv, y_recv, rel_recv,
    dn_send, dn2_send, sib_send, y_send, rel_send, root_send,
    rq_send, rq_recv, rz_send, rz_recv, rg_send, rg_recv, rk_send, rk_recv,
    c_send, c_recv, i_send, i_recv, l_send, l_recv, kq_send, kq_recv, kz_send, kz_recv,
    dn_ready, dn2_ready, z_ready, z_go,
):
    me = lax.axis_index("row")
    col = lax.axis_index("col")
    z = me // 4
    q = lax.rem(me, 4)
    is_root = me == 0
    not_root = jnp.logical_not(is_root)
    heads = col < 2
    at_zero = z == 0
    off_zero = z > 0

    def at_row(r):
        return dict(row=r, col=col)

    z_peers = [at_row(lax.rem(z + d, NZ) * 4 + q) for d in range(1, NZ)]
    q_peers = [at_row(z * 4 + lax.rem(q + d, 4)) for d in range(1, 4)]
    c_peers = [dict(row=me, col=lax.rem(col + d, 8)) for d in range(1, 8)]
    sib_n = q + 1 - 2 * lax.rem(q, 2)
    opp_n = lax.rem(q + 2, 4)
    sib = at_row(z * 4 + sib_n)
    opp = at_row(z * 4 + opp_n)
    has_dn = jnp.logical_and(z != 4, z != 5)
    dn_to = at_row(jnp.where(z < 4, z + 1, jnp.where(has_dn, z - 1, z + 1)) * 4 + q)
    dn2_to = at_row(7 * 4 + q)
    up_from = at_row(jnp.where(z > 4, lax.rem(z + 1, NZ), jnp.where(off_zero, z - 1, z + 1)) * 4 + q)

    def signal(sem, to):
        pl.semaphore_signal(sem, inc=1, device_id=to, device_id_type=MESH)

    loads = [
        pltpu.make_async_copy(a_hbm.at[:, b, :], a_ref.at[b], load_sem.at[b])
        for b in range(4)
    ]
    loads.append(pltpu.make_async_copy(w_hbm, w_ref, load_sem.at[4]))
    loads.append(pltpu.make_async_copy(v_hbm, v_ref, load_sem.at[5]))
    for x in loads:
        x.start()
    panel_load = pltpu.make_async_copy(a_hbm.at[:, 0, :], p_ref, load_sem.at[6])

    @pl.when(is_root)
    def _():
        panel_load.start()

    barrier = pltpu.get_barrier_semaphore()
    for x in q_peers + c_peers:
        signal(barrier, x)

    @pl.when(at_zero)
    def _():
        for x in z_peers:
            signal(barrier, x)

    @pl.when(jnp.logical_and(off_zero, has_dn))
    def _():
        signal(barrier, dn_to)

    pl.semaphore_wait(
        barrier, 10 + jnp.where(at_zero, 0, 1) + jnp.where(jnp.logical_and(z > 1, z < 7), 1, 0)
    )

    @pl.when(off_zero)
    def _():
        @pl.when(z == 7)
        def _():
            signal(dn2_ready, up_from)

        @pl.when(z != 7)
        def _():
            signal(dn_ready, up_from)

        signal(z_ready, at_row(q))

    for x in loads:
        x.wait()

    @pl.when(heads)
    def _():
        mine = pl.ds(pl.multiple_of(col * 64, 64), 64)
        t_ref[:, mine, :] = a_ref[:, 0:64, :]

    def t_copy(part, i, src):
        blocks = pl.ds(0, 1) if part == 0 else pl.ds(1, 3)
        mine = pl.ds(pl.multiple_of(src * 64, 64), 64)
        return pltpu.make_async_remote_copy(
            t_ref.at[blocks, mine, :], t_ref.at[blocks, mine, :],
            t_send.at[part * 7 + i], t_recv.at[part * 2 + src],
            device_id=c_peers[i], device_id_type=MESH,
        )

    @pl.when(heads)
    def _():
        for i in range(7):
            t_copy(0, i, col).start()

    def piece(n, k):
        first = jnp.where(n < 2, n * LONG, 2 * LONG + (n - 2) * SHORT)
        return pl.ds(pl.multiple_of((first + k) * PART, PART), PART)

    def p_copy(n, k, send, recv, to):
        return pltpu.make_async_remote_copy(
            p_ref.at[piece(n, k)], p_ref.at[piece(n, k)],
            send.at[k], recv.at[k], device_id=to, device_id_type=MESH,
        )

    mine_n = jnp.where(q < 2, LONG, SHORT)
    opp_count = LONG + SHORT - mine_n
    to_sib = jnp.logical_not(jnp.logical_and(at_zero, q == 1))
    to_opp = jnp.logical_not(jnp.logical_and(at_zero, q == 2))

    def pass_dn2(k, _):
        p_copy(q, k, dn2_send, own_recv, dn2_to).start()
        return 0

    def pass_quad(k):
        @pl.when(to_opp)
        def _():
            p_copy(q, k, y_send, y_recv, opp).start()

        @pl.when(to_sib)
        def _():
            p_copy(q, k, sib_send, sib_recv, sib).start()

    def pass_opp(k):
        @pl.when(to_sib)
        def _():
            p_copy(opp_n, k, rel_send, rel_recv, sib).start()

    def root_copy(n, k):
        return pltpu.make_async_remote_copy(
            p_ref.at[piece(n, k)], p_ref.at[piece(n, k)],
            root_send.at[(n - 1) * LONG + k], own_recv.at[k],
            device_id=at_row(n), device_id_type=MESH,
        )

    def send_two(k, _):
        p_copy(q, k, dn_send, own_recv, dn_to).start()
        root_copy(1, k).start()
        return 0

    def send_four(k, _):
        root_copy(2, k).start()
        root_copy(3, k).start()
        return send_two(k, 0)

    @pl.when(at_zero)
    def _():
        pl.semaphore_wait(dn_ready, 1)

    @pl.when(is_root)
    def _():
        panel_load.wait()
        lax.fori_loop(0, HEADSTART, send_four, 0)

    def sums(t, acc):
        at = pl.multiple_of(t * 64, 64)
        v = jnp.broadcast_to(v_ref[pl.ds(t, 1), :], (128, 64)).T
        across = jnp.zeros((64, 128), F32)
        out = []
        for b in range(4):
            block = a_ref[b, pl.ds(at, 64), :]
            across = across + block * w_ref[b : b + 1, :]
            out.append(acc[b] + (block * v).reshape(8, 8, 128).sum(0))
        r_ref[pl.ds(t, 1), 0:64] = jnp.sum(across.T, axis=0, keepdims=True)
        return tuple(out)

    r_ref[...] = jnp.zeros((32, 128), F32)
    acc = lax.fori_loop(
        0, 32, sums, tuple(jnp.zeros((8, 128), F32) for _ in range(4)), unroll=4
    )
    for b in range(4):
        c_ref[b : b + 1, :] = jnp.sum(acc[b], axis=0, keepdims=True)
    c_ref[4:8, :] = jnp.zeros((4, 128), F32)

    cz_ref[pl.ds(col, 1)] = c_ref[...][None]

    def c_copy(i):
        return pltpu.make_async_remote_copy(
            cz_ref.at[col], cz_ref.at[col], c_send.at[i], c_recv.at[i],
            device_id=c_peers[i], device_id_type=MESH,
        )

    for i in range(7):
        c_copy(i).start()

    def rq_copy(i):
        to = lax.rem(q + i + 1, 4)
        return pltpu.make_async_remote_copy(
            r_ref.at[pl.ds(pl.multiple_of(to * 8, 8), 8)], rq_ref.at[i],
            rq_send.at[i], rq_recv.at[i],
            device_id=q_peers[i], device_id_type=MESH,
        )

    for i in range(3):
        rq_copy(i).start()

    kq_ref[pl.ds(q, 1)] = r_ref[0:8, :][None]

    def kq_copy(i):
        return pltpu.make_async_remote_copy(
            kq_ref.at[q], kq_ref.at[q], kq_send.at[i], kq_recv.at[i],
            device_id=q_peers[i], device_id_type=MESH,
        )

    def kz_copy(i):
        return pltpu.make_async_remote_copy(
            kz_ref.at[z], kz_ref.at[z], kz_send.at[i], kz_recv.at[i],
            device_id=z_peers[i], device_id_type=MESH,
        )

    def kq_arrival(i):
        return pltpu.make_async_remote_copy(
            kq_ref.at[q], kq_ref.at[lax.rem(q + 3 - i, 4)], kq_send.at[i], kq_recv.at[i],
            device_id=q_peers[i], device_id_type=MESH,
        )

    def kz_arrival(i):
        return pltpu.make_async_remote_copy(
            kz_ref.at[z], kz_ref.at[lax.rem(z + NZ - 1 - i, NZ)], kz_send.at[i], kz_recv.at[i],
            device_id=z_peers[i], device_id_type=MESH,
        )

    @pl.when(heads)
    def _():
        for i in range(3):
            kq_copy(i).start()

    @pl.when(is_root)
    def _():
        lax.fori_loop(HEADSTART, SHORT, send_four, 0)
        lax.fori_loop(SHORT, LONG, send_two, 0)

    @pl.when(heads)
    def _():
        for i in range(7):
            t_copy(1, i, col).start()

    quarter = pl.ds(pl.multiple_of(q * 8, 8), 8)

    def rz_copy(i):
        return pltpu.make_async_remote_copy(
            rz_ref.at[z], rz_ref.at[z], rz_send.at[i], rz_recv.at[i],
            device_id=z_peers[i], device_id_type=MESH,
        )

    def rz_arrival(i):
        return pltpu.make_async_remote_copy(
            rz_ref.at[z], rz_ref.at[lax.rem(z + NZ - 1 - i, NZ)], rz_send.at[i], rz_recv.at[i],
            device_id=z_peers[i], device_id_type=MESH,
        )

    def spread_quarter():
        @pl.when(heads)
        def _():
            for i in range(3):
                kq_copy(i).wait_send()
                kq_arrival(i).wait_recv()
            kz_ref[pl.ds(z, 1)] = (kq_ref[0] + kq_ref[1] + kq_ref[2] + kq_ref[3])[None]
            for i in range(7):
                kz_copy(i).start()

        for i in range(3):
            rq_copy(i).wait()
        total = r_ref[quarter, :] + rq_ref[0] + rq_ref[1] + rq_ref[2]
        rz_ref[pl.ds(z, 1)] = total[None]
        for i in range(7):
            rz_copy(i).start()

    def rg_copy(i):
        return pltpu.make_async_remote_copy(
            rs_ref.at[quarter], rs_ref.at[quarter], rg_send.at[i], rg_recv.at[i],
            device_id=q_peers[i], device_id_type=MESH,
        )

    def rg_arrival(i):
        theirs = pl.ds(pl.multiple_of(lax.rem(q + 3 - i, 4) * 8, 8), 8)
        return pltpu.make_async_remote_copy(
            rs_ref.at[theirs], rs_ref.at[theirs], rg_send.at[i], rg_recv.at[i],
            device_id=q_peers[i], device_id_type=MESH,
        )

    def rk_copy(i):
        return pltpu.make_async_remote_copy(
            rk_ref.at[col], rk_ref.at[col], rk_send.at[i], rk_recv.at[col],
            device_id=c_peers[i], device_id_type=MESH,
        )

    def gather_quarters():
        @pl.when(heads)
        def _():
            for i in range(7):
                kz_arrival(i).wait_recv()
            top = kz_ref[0]
            for i in range(1, 8):
                top = top + kz_ref[i]
            rk_ref[pl.ds(col, 1)] = top[None]
            for i in range(7):
                rk_copy(i).start()

        for i in range(7):
            rz_arrival(i).wait_recv()
        whole = rz_ref[0]
        for i in range(1, 8):
            whole = whole + rz_ref[i]
        rs_ref[quarter, :] = whole
        for i in range(3):
            rg_copy(i).start()

    def take_own(k, _):
        p_copy(q, k, dn_send, own_recv, dn_to).wait_recv()

        @pl.when(has_dn)
        def _():
            p_copy(q, k, dn_send, own_recv, dn_to).start()

        pass_quad(k)
        return 0

    def take_opp(k, _):
        p_copy(opp_n, k, y_send, y_recv, opp).wait_recv()
        pass_opp(k)
        return 0

    def own(a, b):
        lax.fori_loop(a, b, take_own, 0)

    mine = pl.ds(pl.multiple_of(jnp.minimum(col, 1) * 64, 64), 64)

    def i_copy(i, to):
        return pltpu.make_async_remote_copy(
            inv_ref, inv_ref, i_send.at[i], i_recv.at[0], device_id=to, device_id_type=MESH
        )

    def l_copy(i, to):
        return pltpu.make_async_remote_copy(
            rows_ref.at[mine], rows_ref.at[mine], l_send.at[i], l_recv.at[0],
            device_id=to, device_id_type=MESH,
        )

    def inv_to(i, to):
        i_copy(i, to).start()

        @pl.when(heads)
        def _():
            l_copy(i, to).start()

    def inv_wait(i, to):
        i_copy(i, to).wait_send()

        @pl.when(heads)
        def _():
            l_copy(i, to).wait_send()

    even = lax.rem(q, 2) == 0
    over_z = jnp.logical_and(at_zero, even)
    z_order = (0, 6, 1, 5, 2, 4, 3)

    def take_inverse():
        i_copy(0, sib).wait_recv()

        @pl.when(heads)
        def _():
            l_copy(0, sib).wait_recv()

        @pl.when(over_z)
        def _():
            for i in z_order:
                inv_to(i, z_peers[i])

        @pl.when(even)
        def _():
            inv_to(8, sib)

    def sum_columns():
        for i in range(7):
            c_copy(i).wait_recv()
        over = cz_ref[0]
        for i in range(1, 8):
            over = over + cz_ref[i]
        c_ref[...] = over
        return over

    @pl.when(jnp.logical_and(at_zero, not_root))
    def _():
        own(0, 2)

    @pl.when(at_zero)
    def _():
        pl.semaphore_wait(dn2_ready, 1)
        pl.semaphore_wait(z_ready, 7)
        for x in z_peers:
            signal(z_go, x)

    @pl.when(is_root)
    def _():
        lax.fori_loop(0, LONG, pass_dn2, 0)
        spread_quarter()

        def rest(k, _):
            pass_quad(k)
            return 0

        def rest_opp(k, _):
            pass_opp(k)
            return 0

        for s in range(2):
            @pl.when(col != s)
            def _():
                t_copy(0, 0, s).wait_recv()
        eliminate(t_ref.at[0], inv_ref, rows_ref, cols_ref, diag_ref)
        inv_ref[128:136, :] = sum_columns()
        inv_to(7, opp)
        for i in z_order:
            inv_to(i, z_peers[i])
        inv_to(8, sib)
        lax.fori_loop(0, LONG, rest, 0)
        lax.fori_loop(0, SHORT, rest_opp, 0)
        gather_quarters()
        i0 = lax.broadcasted_iota(jnp.int32, (128, 128), 0)
        i1 = lax.broadcasted_iota(jnp.int32, (128, 128), 1)
        inner = diag_ref[...] + jnp.where(i0 == i1, 1.0, 0.0)
        low_ref[...] = jnp.where(i0 // 8 > i1 // 8, -dot(cols_ref[...], inner), inner)

    @pl.when(jnp.logical_and(at_zero, not_root))
    def _():
        lax.fori_loop(0, 2, pass_dn2, 0)
        spread_quarter()

        def both(k, _):
            take_own(k, 0)
            return pass_dn2(k, 0)

        lax.fori_loop(2, mine_n, both, 0)
        gather_quarters()
        take_inverse()
        lax.fori_loop(0, opp_count, take_opp, 0)

    away = jnp.where(z <= 4, z, NZ - z)
    early = mine_n
    before = jnp.where(away <= 1, opp_count, 0)

    @pl.when(off_zero)
    def _():
        pl.semaphore_wait(z_go, 1)
        @pl.when(jnp.logical_and(has_dn, z != 0))
        def _():
            pl.semaphore_wait(dn_ready, 1)

        spread_quarter()

        own(0, early)
        gather_quarters()
        own(early, mine_n)
        lax.fori_loop(0, before, take_opp, 0)
        take_inverse()
        lax.fori_loop(before, opp_count, take_opp, 0)

    @pl.when(not_root)
    def _():
        sum_columns()

    for s in range(2):
        @pl.when(col != s)
        def _():
            @pl.when(not_root)
            def _():
                t_copy(0, 0, s).wait_recv()

            t_copy(1, 0, s).wait_recv()
            pltpu.make_async_remote_copy(
                rk_ref.at[s], rk_ref.at[s], rk_send.at[0], rk_recv.at[s],
                device_id=c_peers[0], device_id_type=MESH,
            ).wait_recv()

    inv = inv_ref[0:128, :]
    crossing = inv_ref[128:136, :]
    for b in range(4):
        at = slice(128 * b, 128 * b + 128)
        c = c_ref[b : b + 1, :]
        if b == 0:
            @pl.when(is_root)
            def _():
                cols_ref[...] = -dot(inv, low_ref[...])

            @pl.when(not_root)
            def _():
                cols_ref[...] = dot(inv, t_ref[0])

            x = cols_ref[...]
            c = jnp.where(is_root, 0.0, c)
        else:
            x = dot(inv, t_ref[b])
        hi = x.astype(BF16)
        xx_ref[0:128, at] = hi
        xx_ref[128:256, at] = hi
        xl_ref[:, at] = (x - hi.astype(F32)).astype(BF16)
        c_ref[b : b + 1, :] = c - dot(crossing, x)[0:1, :]
    rk = jnp.concatenate([rk_ref[0, :, 0:64], rk_ref[1, :, 0:64]], axis=1)
    rk = jnp.broadcast_to(rk[0:1, :], (8, 128))
    xr_ref[:, 0:128] = dot_t(rk, inv)
    for i in range(3):
        rg_arrival(i).wait_recv()
    r_ref[...] = rs_ref[...]

    @pl.when(heads)
    def _():
        i0 = lax.broadcasted_iota(jnp.int32, (64, 128), 0) + col * 64
        i1 = lax.broadcasted_iota(jnp.int32, (64, 128), 1)
        kept = rows_ref[mine, :]
        lin = jnp.where(i0 > i1, kept, jnp.where(i0 == i1, 1.0, 0.0))
        for b in range(4):
            u_ref[b] = dot(lin, t_ref[b])

        @pl.when(is_root)
        def _():
            u_ref[0] = jnp.where(i0 > i1, low_ref[mine, :], kept)

        xr_ref[:, 128:192] = dot_t(rk, lin)

    @pl.when(not_root)
    def _():
        def from_sib(k, _):
            p_copy(sib_n, k, sib_send, sib_recv, sib).wait_recv()
            return 0

        def from_rel(k, _):
            p_copy(lax.rem(sib_n + 2, 4), k, rel_send, rel_recv, sib).wait_recv()
            return 0

        lax.fori_loop(0, mine_n, from_sib, 0)
        lax.fori_loop(0, opp_count, from_rel, 0)

    @pl.when(heads)
    def _():
        for i in range(7):
            t_copy(0, i, col).wait_send()
            t_copy(1, i, col).wait_send()
            rk_copy(i).wait_send()
            kz_copy(i).wait_send()

    for i in range(7):
        c_copy(i).wait_send()
        rz_copy(i).wait_send()
    for i in range(3):
        rg_copy(i).wait_send()

    def sent(k, _):
        @pl.when(has_dn)
        def _():
            p_copy(q, k, dn_send, own_recv, dn_to).wait_send()

        @pl.when(at_zero)
        def _():
            p_copy(q, k, dn2_send, own_recv, dn2_to).wait_send()

        @pl.when(to_opp)
        def _():
            p_copy(q, k, y_send, y_recv, opp).wait_send()

        @pl.when(to_sib)
        def _():
            p_copy(q, k, sib_send, sib_recv, sib).wait_send()

        return 0

    def sent_opp(k, _):
        p_copy(opp_n, k, rel_send, rel_recv, sib).wait_send()
        return 0

    lax.fori_loop(0, mine_n, sent, 0)

    @pl.when(to_sib)
    def _():
        lax.fori_loop(0, opp_count, sent_opp, 0)

    @pl.when(is_root)
    def _():
        def sent_root(k, _):
            root_copy(1, k).wait_send()
            return 0

        def sent_roots(k, _):
            root_copy(2, k).wait_send()
            root_copy(3, k).wait_send()
            return 0

        lax.fori_loop(0, LONG, sent_root, 0)
        lax.fori_loop(0, SHORT, sent_roots, 0)

    @pl.when(over_z)
    def _():
        for i in range(7):
            inv_wait(i, z_peers[i])

    @pl.when(is_root)
    def _():
        inv_wait(7, opp)

    @pl.when(even)
    def _():
        inv_wait(8, sib)


def update(
    a_ref, p_ref, xx_ref, xl_ref, xr_ref, u_ref, r_ref, c_ref, o_ref, ro_ref, co_ref
):
    step = pl.program_id(0)
    me = lax.axis_index("row")
    col = lax.axis_index("col")
    rows = a_ref.shape[0] // 4
    p = p_ref[...]
    hi = p.astype(BF16)
    lo = (p - hi.astype(F32)).astype(BF16)
    both = jnp.concatenate([hi, lo], axis=1)
    d = jnp.dot(both, xx_ref[...], preferred_element_type=F32)
    d = d + jnp.dot(hi, xl_ref[...], preferred_element_type=F32)
    for b in range(4):
        a = a_ref[pl.ds(b, rows, 4), :]
        if b == 0:
            a = jnp.where(me == 0, 0.0, a)
        o_ref[pl.ds(b, rows, 4), :] = a - d[:, 128 * b : 128 * b + 128]
    x = xr_ref[:, 0:128]
    xh = x.astype(BF16)
    xw = (x - xh.astype(F32)).astype(BF16)
    nt = (((1,), (1,)), ((), ()))
    pair = jnp.concatenate([xh, xw], axis=0)
    e = lax.dot_general(pair, hi, nt, preferred_element_type=F32)
    e = e[0:1, :] + e[8:9, :] + lax.dot_general(xh, lo, nt, preferred_element_type=F32)[0:1, :]
    for t in range(rows // 64):
        at = step * (rows // 64) + t
        ro_ref[pl.ds(at, 1), :] = r_ref[pl.ds(at, 1), 0:64] - e[:, 64 * t : 64 * t + 64]

    @pl.when(step == 0)
    def _():
        co_ref[...] = c_ref[0:4, :]

        @pl.when(col < 2)
        def _():
            for b in range(4):
                o_ref[pl.ds(b, 64, 4), :] = u_ref[b]
            ro_ref[0:1, :] = xr_ref[0:1, 128:192]


def in_hbm(x):
    return pltpu.with_memory_space_constraint(x, pltpu.HBM)


def per_device(matrix, column_weight, row_weight):
    n_rows = matrix.shape[0] * matrix.shape[2]
    dma = pltpu.SemaphoreType.DMA
    outs = [
        ((n_rows, 128), F32), ((256, 512), BF16), ((128, 512), BF16), ((8, 256), F32),
        ((4, 64, 128), F32), ((32, 128), F32), ((8, 128), F32),
    ]
    vmem = pl.BlockSpec(memory_space=pltpu.VMEM)
    got = pl.pallas_call(
        exchange,
        out_shape=[jax.ShapeDtypeStruct(*s) for s in outs],
        in_specs=[pl.BlockSpec(memory_space=pltpu.HBM)] * 3,
        out_specs=[vmem] * len(outs),
        scratch_shapes=[
            pltpu.VMEM((4, 128, 128), F32),
            pltpu.VMEM((136, 128), F32),
            pltpu.VMEM((128, 128), F32),
            pltpu.VMEM((128, 128), F32),
            pltpu.VMEM((2, 8, 128), F32),
            pltpu.VMEM((128, 128), F32),
            pltpu.VMEM((128, 128), F32),
            pltpu.VMEM((4, n_rows, 128), F32),
            pltpu.VMEM((4, 128), F32),
            pltpu.VMEM((32, 64), F32),
            pltpu.VMEM((3, 8, 128), F32),
            pltpu.VMEM((8, 8, 128), F32),
            pltpu.VMEM((32, 128), F32),
            pltpu.VMEM((8, 8, 128), F32),
            pltpu.VMEM((4, 8, 128), F32),
            pltpu.VMEM((8, 8, 128), F32),
            dma((7,)), dma((14,)), dma((4,)),
            dma((LONG,)), dma((LONG,)), dma((LONG,)), dma((LONG,)),
            dma((LONG,)), dma((LONG,)), dma((LONG,)), dma((LONG,)), dma((LONG,)), dma((3 * LONG,)),
            dma((3,)), dma((3,)), dma((7,)), dma((7,)), dma((3,)), dma((3,)),
            dma((7,)), dma((2,)), dma((7,)), dma((7,)), dma((9,)), dma((1,)),
            dma((9,)), dma((1,)), dma((3,)), dma((3,)), dma((7,)), dma((7,)),
        ]
        + [pltpu.SemaphoreType.REGULAR] * 4,
        compiler_params=pltpu.CompilerParams(
            collective_id=0, has_side_effects=True, vmem_limit_bytes=24 << 20
        ),
        name="exchange",
    )(
        in_hbm(matrix.reshape(n_rows, 4, 128)),
        in_hbm(column_weight.reshape(4, 128)),
        in_hbm(row_weight.reshape(32, 64)),
    )
    rows = n_rows // STEPS
    whole = lambda s: pl.BlockSpec(s, lambda i: (0,) * len(s))
    out, r, c = pl.pallas_call(
        update,
        grid=(STEPS,),
        out_shape=[
            jax.ShapeDtypeStruct((n_rows * 4, 128), F32),
            jax.ShapeDtypeStruct((32, 64), F32),
            jax.ShapeDtypeStruct((4, 128), F32),
        ],
        in_specs=[
            pl.BlockSpec((rows * 4, 128), lambda i: (i, 0)),
            pl.BlockSpec((rows, 128), lambda i: (i, 0)),
        ]
        + [whole(s) for s, _ in outs[1:]],
        out_specs=[
            pl.BlockSpec((rows * 4, 128), lambda i: (i, 0)),
            whole((32, 64)),
            whole((4, 128)),
        ],
        compiler_params=pltpu.CompilerParams(vmem_limit_bytes=24 << 20),
        name="update",
    )(matrix.reshape(n_rows * 4, 128), *got)
    return (
        out.reshape(matrix.shape),
        r.reshape(row_weight.shape),
        c.reshape(column_weight.shape),
    )


def solution(mesh):
    return jax.shard_map(
        per_device,
        mesh=mesh,
        in_specs=(
            P(None, "col", None, None, "row", None),
            P(None, "row", None),
            P(None, "col", None),
        ),
        out_specs=(
            P(None, "col", None, None, "row", None),
            P(None, "col", None),
            P(None, "row", None),
        ),
        check_vma=False,
    )
```

```python
import jax
import jax.numpy as jnp
from jax import lax
from jax.experimental import pallas as pl
from jax.experimental.pallas import tpu as pltpu
from jax.sharding import PartitionSpec as P

MESH = pl.DeviceIdType.MESH
highest = lax.Precision.HIGH
F32 = jnp.float32
BF16 = jnp.bfloat16
NZ = 8
PART = 64
LONG = 10
SHORT = 6
HEADSTART = 4
STEPS = 2


def dot(a, b):
    return jnp.dot(a, b, precision=highest, preferred_element_type=F32)


def dot_t(a, b):
    return lax.dot_general(
        a, b, (((1,), (1,)), ((), ())), precision=highest, preferred_element_type=F32
    )


def eliminate(g_ref, inv_ref, rows_ref, cols_ref, diag_ref):
    lane = lax.broadcasted_iota(jnp.int32, (8, 128), 1)
    sub = lax.broadcasted_iota(jnp.int32, (8, 128), 0)
    full = (8, 128)
    vs = [g_ref[8 * j : 8 * j + 8, :] for j in range(16)]
    kept_cols = [jnp.zeros(full, F32) for _ in range(16)]
    for s in range(16):
        base = 8 * s
        inside = jnp.logical_and(lane >= base, lane < base + 8)
        v0 = vs[s]
        cs = [jnp.broadcast_to(v0[:, base + j : base + j + 1], full) for j in range(8)]
        factors = [
            [jnp.broadcast_to(vs[r][:, base + j : base + j + 1], full) for j in range(8)]
            if r != s else None
            for r in range(16)
        ]
        v = v0
        diag = jnp.zeros(full, F32)
        for i in range(8):
            here = lane == base + i
            at_i = sub == i
            under = sub > i
            recip = 1.0 / jnp.broadcast_to(cs[i][i : i + 1, :], full)
            ratio = cs[i] * recip
            down = jnp.where(under, ratio, 0.0)
            row = jnp.broadcast_to(v[i : i + 1, :], full)
            v = jnp.where(jnp.logical_and(here, under), -ratio, v - down * jnp.where(here, 0.0, row))
            diag = jnp.where(here, down, diag)
            for j in range(8):
                if j != i:
                    t = jnp.broadcast_to(cs[j][i : i + 1, :], full)
                    cs[j] = jnp.where(at_i, t * recip, cs[j] - ratio * t)
            cs[i] = jnp.where(at_i, recip, -ratio)
        rows_ref[base : base + 8, :] = v
        diag_ref[base : base + 8, :] = diag
        v0 = jnp.where(inside, jnp.where(lane - base == sub, 1.0, 0.0), v0)
        w = cs[0] * jnp.broadcast_to(v0[0:1, :], full)
        for j in range(1, 8):
            w = w + cs[j] * jnp.broadcast_to(v0[j : j + 1, :], full)
        wr = [jnp.broadcast_to(w[j : j + 1, :], full) for j in range(8)]
        order = [r % 16 for r in range(s + 1, s + 16)]
        for r in order:
            f = factors[r]
            a = f[0] * wr[0] + f[1] * wr[1]
            b = f[2] * wr[2] + f[3] * wr[3]
            c = f[4] * wr[4] + f[5] * wr[5]
            d = f[6] * wr[6] + f[7] * wr[7]
            new = jnp.where(inside, 0.0, vs[r]) - ((a + b) + (c + d))
            vs[r] = new
            if r > s:
                kept_cols[r] = jnp.where(inside, new, kept_cols[r])
        vs[s] = w
    for j in range(16):
        inv_ref[8 * j : 8 * j + 8, :] = vs[j]
        cols_ref[8 * j : 8 * j + 8, :] = kept_cols[j]


def exchange(
    a_hbm, w_hbm, v_hbm,
    p_ref, xx_ref, xl_ref, xr_ref, u_ref, r_ref, c_ref,
    t_ref, inv_ref, rows_ref, low_ref, rk_ref,
    cols_ref, diag_ref, a_ref, w_ref, v_ref, rq_ref, rz_ref, rs_ref, cz_ref, kq_ref, kz_ref,
    load_sem, t_send, t_recv, own_recv, sib_recv, y_recv, rel_recv,
    dn_send, dn2_send, sib_send, y_send, rel_send, root_send,
    rq_send, rq_recv, rz_send, rz_recv, rg_send, rg_recv, rk_send, rk_recv,
    c_send, c_recv, i_send, i_recv, l_send, l_recv, kq_send, kq_recv, kz_send, kz_recv,
    dn_ready, dn2_ready, z_ready, z_go,
):
    me = lax.axis_index("row")
    col = lax.axis_index("col")
    z = me // 4
    q = lax.rem(me, 4)
    is_root = me == 0
    not_root = jnp.logical_not(is_root)
    heads = col < 2
    at_zero = z == 0
    off_zero = z > 0

    def at_row(r):
        return dict(row=r, col=col)

    z_peers = [at_row(lax.rem(z + d, NZ) * 4 + q) for d in range(1, NZ)]
    q_peers = [at_row(z * 4 + lax.rem(q + d, 4)) for d in range(1, 4)]
    c_peers = [dict(row=me, col=lax.rem(col + d, 8)) for d in range(1, 8)]
    sib_n = q + 1 - 2 * lax.rem(q, 2)
    opp_n = lax.rem(q + 2, 4)
    sib = at_row(z * 4 + sib_n)
    opp = at_row(z * 4 + opp_n)
    has_dn = jnp.logical_and(z != 4, z != 5)
    dn_to = at_row(jnp.where(z < 4, z + 1, jnp.where(has_dn, z - 1, z + 1)) * 4 + q)
    dn2_to = at_row(7 * 4 + q)
    up_from = at_row(jnp.where(z > 4, lax.rem(z + 1, NZ), jnp.where(off_zero, z - 1, z + 1)) * 4 + q)

    def signal(sem, to):
        pl.semaphore_signal(sem, inc=1, device_id=to, device_id_type=MESH)

    loads = [
        pltpu.make_async_copy(a_hbm.at[:, b, :], a_ref.at[b], load_sem.at[b])
        for b in range(4)
    ]
    loads.append(pltpu.make_async_copy(w_hbm, w_ref, load_sem.at[4]))
    loads.append(pltpu.make_async_copy(v_hbm, v_ref, load_sem.at[5]))
    for x in loads:
        x.start()
    panel_load = pltpu.make_async_copy(a_hbm.at[:, 0, :], p_ref, load_sem.at[6])

    @pl.when(is_root)
    def _():
        panel_load.start()

    barrier = pltpu.get_barrier_semaphore()
    for x in q_peers + c_peers:
        signal(barrier, x)

    @pl.when(at_zero)
    def _():
        for x in z_peers:
            signal(barrier, x)

    @pl.when(jnp.logical_and(off_zero, has_dn))
    def _():
        signal(barrier, dn_to)

    pl.semaphore_wait(
        barrier, 10 + jnp.where(at_zero, 0, 1) + jnp.where(jnp.logical_and(z > 1, z < 7), 1, 0)
    )

    @pl.when(off_zero)
    def _():
        @pl.when(z == 7)
        def _():
            signal(dn2_ready, up_from)

        @pl.when(z != 7)
        def _():
            signal(dn_ready, up_from)

        signal(z_ready, at_row(q))

    for x in loads:
        x.wait()

    @pl.when(heads)
    def _():
        mine = pl.ds(pl.multiple_of(col * 64, 64), 64)
        t_ref[:, mine, :] = a_ref[:, 0:64, :]

    def t_copy(part, i, src):
        blocks = pl.ds(0, 1) if part == 0 else pl.ds(1, 3)
        mine = pl.ds(pl.multiple_of(src * 64, 64), 64)
        return pltpu.make_async_remote_copy(
            t_ref.at[blocks, mine, :], t_ref.at[blocks, mine, :],
            t_send.at[part * 7 + i], t_recv.at[part * 2 + src],
            device_id=c_peers[i], device_id_type=MESH,
        )

    @pl.when(heads)
    def _():
        for i in range(7):
            t_copy(0, i, col).start()

    def piece(n, k):
        first = jnp.where(n < 2, n * LONG, 2 * LONG + (n - 2) * SHORT)
        return pl.ds(pl.multiple_of((first + k) * PART, PART), PART)

    def p_copy(n, k, send, recv, to):
        return pltpu.make_async_remote_copy(
            p_ref.at[piece(n, k)], p_ref.at[piece(n, k)],
            send.at[k], recv.at[k], device_id=to, device_id_type=MESH,
        )

    mine_n = jnp.where(q < 2, LONG, SHORT)
    opp_count = LONG + SHORT - mine_n
    to_sib = jnp.logical_not(jnp.logical_and(at_zero, q == 1))
    to_opp = jnp.logical_not(jnp.logical_and(at_zero, q == 2))

    def pass_dn2(k, _):
        p_copy(q, k, dn2_send, own_recv, dn2_to).start()
        return 0

    def pass_quad(k):
        @pl.when(to_opp)
        def _():
            p_copy(q, k, y_send, y_recv, opp).start()

        @pl.when(to_sib)
        def _():
            p_copy(q, k, sib_send, sib_recv, sib).start()

    def pass_opp(k):
        @pl.when(to_sib)
        def _():
            p_copy(opp_n, k, rel_send, rel_recv, sib).start()

    def root_copy(n, k):
        return pltpu.make_async_remote_copy(
            p_ref.at[piece(n, k)], p_ref.at[piece(n, k)],
            root_send.at[(n - 1) * LONG + k], own_recv.at[k],
            device_id=at_row(n), device_id_type=MESH,
        )

    def send_two(k, _):
        p_copy(q, k, dn_send, own_recv, dn_to).start()
        root_copy(1, k).start()
        return 0

    def send_four(k, _):
        root_copy(2, k).start()
        root_copy(3, k).start()
        return send_two(k, 0)

    @pl.when(at_zero)
    def _():
        pl.semaphore_wait(dn_ready, 1)

    @pl.when(is_root)
    def _():
        panel_load.wait()
        lax.fori_loop(0, HEADSTART, send_four, 0)

    def sums(t, acc):
        at = pl.multiple_of(t * 64, 64)
        v = jnp.broadcast_to(v_ref[pl.ds(t, 1), :], (128, 64)).T
        across = jnp.zeros((64, 128), F32)
        out = []
        for b in range(4):
            block = a_ref[b, pl.ds(at, 64), :]
            across = across + block * w_ref[b : b + 1, :]
            out.append(acc[b] + (block * v).reshape(8, 8, 128).sum(0))
        r_ref[pl.ds(t, 1), 0:64] = jnp.sum(across.T, axis=0, keepdims=True)
        return tuple(out)

    r_ref[...] = jnp.zeros((32, 128), F32)
    acc = lax.fori_loop(
        0, 32, sums, tuple(jnp.zeros((8, 128), F32) for _ in range(4)), unroll=4
    )
    for b in range(4):
        c_ref[b : b + 1, :] = jnp.sum(acc[b], axis=0, keepdims=True)
    c_ref[4:8, :] = jnp.zeros((4, 128), F32)

    cz_ref[pl.ds(col, 1)] = c_ref[...][None]

    def c_copy(i):
        return pltpu.make_async_remote_copy(
            cz_ref.at[col], cz_ref.at[col], c_send.at[i], c_recv.at[i],
            device_id=c_peers[i], device_id_type=MESH,
        )

    for i in range(7):
        c_copy(i).start()

    def rq_copy(i):
        to = lax.rem(q + i + 1, 4)
        return pltpu.make_async_remote_copy(
            r_ref.at[pl.ds(pl.multiple_of(to * 8, 8), 8)], rq_ref.at[i],
            rq_send.at[i], rq_recv.at[i],
            device_id=q_peers[i], device_id_type=MESH,
        )

    for i in range(3):
        rq_copy(i).start()

    kq_ref[pl.ds(q, 1)] = r_ref[0:8, :][None]

    def kq_copy(i):
        return pltpu.make_async_remote_copy(
            kq_ref.at[q], kq_ref.at[q], kq_send.at[i], kq_recv.at[i],
            device_id=q_peers[i], device_id_type=MESH,
        )

    def kz_copy(i):
        return pltpu.make_async_remote_copy(
            kz_ref.at[z], kz_ref.at[z], kz_send.at[i], kz_recv.at[i],
            device_id=z_peers[i], device_id_type=MESH,
        )

    def kq_arrival(i):
        return pltpu.make_async_remote_copy(
            kq_ref.at[q], kq_ref.at[lax.rem(q + 3 - i, 4)], kq_send.at[i], kq_recv.at[i],
            device_id=q_peers[i], device_id_type=MESH,
        )

    def kz_arrival(i):
        return pltpu.make_async_remote_copy(
            kz_ref.at[z], kz_ref.at[lax.rem(z + NZ - 1 - i, NZ)], kz_send.at[i], kz_recv.at[i],
            device_id=z_peers[i], device_id_type=MESH,
        )

    @pl.when(heads)
    def _():
        for i in range(3):
            kq_copy(i).start()

    @pl.when(is_root)
    def _():
        lax.fori_loop(HEADSTART, SHORT, send_four, 0)
        lax.fori_loop(SHORT, LONG, send_two, 0)

    @pl.when(heads)
    def _():
        for i in range(7):
            t_copy(1, i, col).start()

    quarter = pl.ds(pl.multiple_of(q * 8, 8), 8)

    def rz_copy(i):
        return pltpu.make_async_remote_copy(
            rz_ref.at[z], rz_ref.at[z], rz_send.at[i], rz_recv.at[i],
            device_id=z_peers[i], device_id_type=MESH,
        )

    def rz_arrival(i):
        return pltpu.make_async_remote_copy(
            rz_ref.at[z], rz_ref.at[lax.rem(z + NZ - 1 - i, NZ)], rz_send.at[i], rz_recv.at[i],
            device_id=z_peers[i], device_id_type=MESH,
        )

    def spread_quarter():
        @pl.when(heads)
        def _():
            for i in range(3):
                kq_copy(i).wait_send()
                kq_arrival(i).wait_recv()
            kz_ref[pl.ds(z, 1)] = (kq_ref[0] + kq_ref[1] + kq_ref[2] + kq_ref[3])[None]
            for i in range(7):
                kz_copy(i).start()

        for i in range(3):
            rq_copy(i).wait()
        total = r_ref[quarter, :] + rq_ref[0] + rq_ref[1] + rq_ref[2]
        rz_ref[pl.ds(z, 1)] = total[None]
        for i in range(7):
            rz_copy(i).start()

    def rg_copy(i):
        return pltpu.make_async_remote_copy(
            rs_ref.at[quarter], rs_ref.at[quarter], rg_send.at[i], rg_recv.at[i],
            device_id=q_peers[i], device_id_type=MESH,
        )

    def rg_arrival(i):
        theirs = pl.ds(pl.multiple_of(lax.rem(q + 3 - i, 4) * 8, 8), 8)
        return pltpu.make_async_remote_copy(
            rs_ref.at[theirs], rs_ref.at[theirs], rg_send.at[i], rg_recv.at[i],
            device_id=q_peers[i], device_id_type=MESH,
        )

    def rk_copy(i):
        return pltpu.make_async_remote_copy(
            rk_ref.at[col], rk_ref.at[col], rk_send.at[i], rk_recv.at[col],
            device_id=c_peers[i], device_id_type=MESH,
        )

    def gather_quarters():
        @pl.when(heads)
        def _():
            for i in range(7):
                kz_arrival(i).wait_recv()
            top = kz_ref[0]
            for i in range(1, 8):
                top = top + kz_ref[i]
            rk_ref[pl.ds(col, 1)] = top[None]
            for i in range(7):
                rk_copy(i).start()

        for i in range(7):
            rz_arrival(i).wait_recv()
        whole = rz_ref[0]
        for i in range(1, 8):
            whole = whole + rz_ref[i]
        rs_ref[quarter, :] = whole
        for i in range(3):
            rg_copy(i).start()

    def take_own(k, _):
        p_copy(q, k, dn_send, own_recv, dn_to).wait_recv()

        @pl.when(has_dn)
        def _():
            p_copy(q, k, dn_send, own_recv, dn_to).start()

        pass_quad(k)
        return 0

    def take_opp(k, _):
        p_copy(opp_n, k, y_send, y_recv, opp).wait_recv()
        pass_opp(k)
        return 0

    def own(a, b):
        lax.fori_loop(a, b, take_own, 0)

    mine = pl.ds(pl.multiple_of(jnp.minimum(col, 1) * 64, 64), 64)

    def i_copy(i, to):
        return pltpu.make_async_remote_copy(
            inv_ref, inv_ref, i_send.at[i], i_recv.at[0], device_id=to, device_id_type=MESH
        )

    def l_copy(i, to):
        return pltpu.make_async_remote_copy(
            rows_ref.at[mine], rows_ref.at[mine], l_send.at[i], l_recv.at[0],
            device_id=to, device_id_type=MESH,
        )

    def inv_to(i, to):
        i_copy(i, to).start()

        @pl.when(heads)
        def _():
            l_copy(i, to).start()

    def inv_wait(i, to):
        i_copy(i, to).wait_send()

        @pl.when(heads)
        def _():
            l_copy(i, to).wait_send()

    even = lax.rem(q, 2) == 0
    over_z = jnp.logical_and(at_zero, even)
    z_order = (0, 6, 1, 5, 2, 4, 3)

    def take_inverse():
        i_copy(0, sib).wait_recv()

        @pl.when(heads)
        def _():
            l_copy(0, sib).wait_recv()

        @pl.when(over_z)
        def _():
            for i in z_order:
                inv_to(i, z_peers[i])

        @pl.when(even)
        def _():
            inv_to(8, sib)

    def sum_columns():
        for i in range(7):
            c_copy(i).wait_recv()
        over = cz_ref[0]
        for i in range(1, 8):
            over = over + cz_ref[i]
        c_ref[...] = over
        return over

    @pl.when(jnp.logical_and(at_zero, not_root))
    def _():
        own(0, 1)

    @pl.when(at_zero)
    def _():
        pl.semaphore_wait(dn2_ready, 1)
        pl.semaphore_wait(z_ready, 7)
        for x in z_peers:
            signal(z_go, x)

    @pl.when(is_root)
    def _():
        lax.fori_loop(0, LONG, pass_dn2, 0)
        spread_quarter()

        def rest(k, _):
            pass_quad(k)
            return 0

        def rest_opp(k, _):
            pass_opp(k)
            return 0

        for s in range(2):
            @pl.when(col != s)
            def _():
                t_copy(0, 0, s).wait_recv()
        eliminate(t_ref.at[0], inv_ref, rows_ref, cols_ref, diag_ref)
        inv_ref[128:136, :] = sum_columns()
        inv_to(7, opp)
        for i in z_order:
            inv_to(i, z_peers[i])
        inv_to(8, sib)
        lax.fori_loop(0, LONG, rest, 0)
        lax.fori_loop(0, SHORT, rest_opp, 0)
        gather_quarters()
        i0 = lax.broadcasted_iota(jnp.int32, (128, 128), 0)
        i1 = lax.broadcasted_iota(jnp.int32, (128, 128), 1)
        inner = diag_ref[...] + jnp.where(i0 == i1, 1.0, 0.0)
        low_ref[...] = jnp.where(i0 // 8 > i1 // 8, -dot(cols_ref[...], inner), inner)

    @pl.when(jnp.logical_and(at_zero, not_root))
    def _():
        lax.fori_loop(0, 1, pass_dn2, 0)
        spread_quarter()

        def both(k, _):
            take_own(k, 0)
            return pass_dn2(k, 0)

        lax.fori_loop(1, mine_n, both, 0)
        gather_quarters()
        take_inverse()
        lax.fori_loop(0, opp_count, take_opp, 0)

    away = jnp.where(z <= 4, z, NZ - z)
    early = mine_n
    before = jnp.where(away <= 1, opp_count, 0)

    @pl.when(off_zero)
    def _():
        pl.semaphore_wait(z_go, 1)
        @pl.when(jnp.logical_and(has_dn, z != 0))
        def _():
            pl.semaphore_wait(dn_ready, 1)

        spread_quarter()

        own(0, early)
        gather_quarters()
        own(early, mine_n)
        lax.fori_loop(0, before, take_opp, 0)
        take_inverse()
        lax.fori_loop(before, opp_count, take_opp, 0)

    @pl.when(not_root)
    def _():
        sum_columns()

    for s in range(2):
        @pl.when(col != s)
        def _():
            @pl.when(not_root)
            def _():
                t_copy(0, 0, s).wait_recv()

            t_copy(1, 0, s).wait_recv()
            pltpu.make_async_remote_copy(
                rk_ref.at[s], rk_ref.at[s], rk_send.at[0], rk_recv.at[s],
                device_id=c_peers[0], device_id_type=MESH,
            ).wait_recv()

    inv = inv_ref[0:128, :]
    crossing = inv_ref[128:136, :]
    for b in range(4):
        at = slice(128 * b, 128 * b + 128)
        c = c_ref[b : b + 1, :]
        if b == 0:
            @pl.when(is_root)
            def _():
                cols_ref[...] = -dot(inv, low_ref[...])

            @pl.when(not_root)
            def _():
                cols_ref[...] = dot(inv, t_ref[0])

            x = cols_ref[...]
            c = jnp.where(is_root, 0.0, c)
        else:
            x = dot(inv, t_ref[b])
        hi = x.astype(BF16)
        xx_ref[0:128, at] = hi
        xx_ref[128:256, at] = hi
        xl_ref[:, at] = (x - hi.astype(F32)).astype(BF16)
        c_ref[b : b + 1, :] = c - dot(crossing, x)[0:1, :]
    rk = jnp.concatenate([rk_ref[0, :, 0:64], rk_ref[1, :, 0:64]], axis=1)
    rk = jnp.broadcast_to(rk[0:1, :], (8, 128))
    xr_ref[:, 0:128] = dot_t(rk, inv)
    for i in range(3):
        rg_arrival(i).wait_recv()
    r_ref[...] = rs_ref[...]

    @pl.when(heads)
    def _():
        i0 = lax.broadcasted_iota(jnp.int32, (64, 128), 0) + col * 64
        i1 = lax.broadcasted_iota(jnp.int32, (64, 128), 1)
        kept = rows_ref[mine, :]
        lin = jnp.where(i0 > i1, kept, jnp.where(i0 == i1, 1.0, 0.0))
        for b in range(4):
            u_ref[b] = dot(lin, t_ref[b])

        @pl.when(is_root)
        def _():
            u_ref[0] = jnp.where(i0 > i1, low_ref[mine, :], kept)

        xr_ref[:, 128:192] = dot_t(rk, lin)

    @pl.when(not_root)
    def _():
        def from_sib(k, _):
            p_copy(sib_n, k, sib_send, sib_recv, sib).wait_recv()
            return 0

        def from_rel(k, _):
            p_copy(lax.rem(sib_n + 2, 4), k, rel_send, rel_recv, sib).wait_recv()
            return 0

        lax.fori_loop(0, mine_n, from_sib, 0)
        lax.fori_loop(0, opp_count, from_rel, 0)

    @pl.when(heads)
    def _():
        for i in range(7):
            t_copy(0, i, col).wait_send()
            t_copy(1, i, col).wait_send()
            rk_copy(i).wait_send()
            kz_copy(i).wait_send()

    for i in range(7):
        c_copy(i).wait_send()
        rz_copy(i).wait_send()
    for i in range(3):
        rg_copy(i).wait_send()

    def sent(k, _):
        @pl.when(has_dn)
        def _():
            p_copy(q, k, dn_send, own_recv, dn_to).wait_send()

        @pl.when(at_zero)
        def _():
            p_copy(q, k, dn2_send, own_recv, dn2_to).wait_send()

        @pl.when(to_opp)
        def _():
            p_copy(q, k, y_send, y_recv, opp).wait_send()

        @pl.when(to_sib)
        def _():
            p_copy(q, k, sib_send, sib_recv, sib).wait_send()

        return 0

    def sent_opp(k, _):
        p_copy(opp_n, k, rel_send, rel_recv, sib).wait_send()
        return 0

    lax.fori_loop(0, mine_n, sent, 0)

    @pl.when(to_sib)
    def _():
        lax.fori_loop(0, opp_count, sent_opp, 0)

    @pl.when(is_root)
    def _():
        def sent_root(k, _):
            root_copy(1, k).wait_send()
            return 0

        def sent_roots(k, _):
            root_copy(2, k).wait_send()
            root_copy(3, k).wait_send()
            return 0

        lax.fori_loop(0, LONG, sent_root, 0)
        lax.fori_loop(0, SHORT, sent_roots, 0)

    @pl.when(over_z)
    def _():
        for i in range(7):
            inv_wait(i, z_peers[i])

    @pl.when(is_root)
    def _():
        inv_wait(7, opp)

    @pl.when(even)
    def _():
        inv_wait(8, sib)


def update(
    a_ref, p_ref, xx_ref, xl_ref, xr_ref, u_ref, r_ref, c_ref, o_ref, ro_ref, co_ref
):
    step = pl.program_id(0)
    me = lax.axis_index("row")
    col = lax.axis_index("col")
    rows = a_ref.shape[0] // 4
    p = p_ref[...]
    hi = p.astype(BF16)
    lo = (p - hi.astype(F32)).astype(BF16)
    both = jnp.concatenate([hi, lo], axis=1)
    d = jnp.dot(both, xx_ref[...], preferred_element_type=F32)
    d = d + jnp.dot(hi, xl_ref[...], preferred_element_type=F32)
    for b in range(4):
        a = a_ref[pl.ds(b, rows, 4), :]
        if b == 0:
            a = jnp.where(me == 0, 0.0, a)
        o_ref[pl.ds(b, rows, 4), :] = a - d[:, 128 * b : 128 * b + 128]
    x = xr_ref[:, 0:128]
    xh = x.astype(BF16)
    xw = (x - xh.astype(F32)).astype(BF16)
    nt = (((1,), (1,)), ((), ()))
    pair = jnp.concatenate([xh, xw], axis=0)
    e = lax.dot_general(pair, hi, nt, preferred_element_type=F32)
    e = e[0:1, :] + e[8:9, :] + lax.dot_general(xh, lo, nt, preferred_element_type=F32)[0:1, :]
    for t in range(rows // 64):
        at = step * (rows // 64) + t
        ro_ref[pl.ds(at, 1), :] = r_ref[pl.ds(at, 1), 0:64] - e[:, 64 * t : 64 * t + 64]

    @pl.when(step == 0)
    def _():
        co_ref[...] = c_ref[0:4, :]

        @pl.when(col < 2)
        def _():
            for b in range(4):
                o_ref[pl.ds(b, 64, 4), :] = u_ref[b]
            ro_ref[0:1, :] = xr_ref[0:1, 128:192]


def in_hbm(x):
    return pltpu.with_memory_space_constraint(x, pltpu.HBM)


def per_device(matrix, column_weight, row_weight):
    n_rows = matrix.shape[0] * matrix.shape[2]
    dma = pltpu.SemaphoreType.DMA
    outs = [
        ((n_rows, 128), F32), ((256, 512), BF16), ((128, 512), BF16), ((8, 256), F32),
        ((4, 64, 128), F32), ((32, 128), F32), ((8, 128), F32),
    ]
    vmem = pl.BlockSpec(memory_space=pltpu.VMEM)
    got = pl.pallas_call(
        exchange,
        out_shape=[jax.ShapeDtypeStruct(*s) for s in outs],
        in_specs=[pl.BlockSpec(memory_space=pltpu.HBM)] * 3,
        out_specs=[vmem] * len(outs),
        scratch_shapes=[
            pltpu.VMEM((4, 128, 128), F32),
            pltpu.VMEM((136, 128), F32),
            pltpu.VMEM((128, 128), F32),
            pltpu.VMEM((128, 128), F32),
            pltpu.VMEM((2, 8, 128), F32),
            pltpu.VMEM((128, 128), F32),
            pltpu.VMEM((128, 128), F32),
            pltpu.VMEM((4, n_rows, 128), F32),
            pltpu.VMEM((4, 128), F32),
            pltpu.VMEM((32, 64), F32),
            pltpu.VMEM((3, 8, 128), F32),
            pltpu.VMEM((8, 8, 128), F32),
            pltpu.VMEM((32, 128), F32),
            pltpu.VMEM((8, 8, 128), F32),
            pltpu.VMEM((4, 8, 128), F32),
            pltpu.VMEM((8, 8, 128), F32),
            dma((7,)), dma((14,)), dma((4,)),
            dma((LONG,)), dma((LONG,)), dma((LONG,)), dma((LONG,)),
            dma((LONG,)), dma((LONG,)), dma((LONG,)), dma((LONG,)), dma((LONG,)), dma((3 * LONG,)),
            dma((3,)), dma((3,)), dma((7,)), dma((7,)), dma((3,)), dma((3,)),
            dma((7,)), dma((2,)), dma((7,)), dma((7,)), dma((9,)), dma((1,)),
            dma((9,)), dma((1,)), dma((3,)), dma((3,)), dma((7,)), dma((7,)),
        ]
        + [pltpu.SemaphoreType.REGULAR] * 4,
        compiler_params=pltpu.CompilerParams(
            collective_id=0, has_side_effects=True, vmem_limit_bytes=24 << 20
        ),
        name="exchange",
    )(
        in_hbm(matrix.reshape(n_rows, 4, 128)),
        in_hbm(column_weight.reshape(4, 128)),
        in_hbm(row_weight.reshape(32, 64)),
    )
    rows = n_rows // STEPS
    whole = lambda s: pl.BlockSpec(s, lambda i: (0,) * len(s))
    out, r, c = pl.pallas_call(
        update,
        grid=(STEPS,),
        out_shape=[
            jax.ShapeDtypeStruct((n_rows * 4, 128), F32),
            jax.ShapeDtypeStruct((32, 64), F32),
            jax.ShapeDtypeStruct((4, 128), F32),
        ],
        in_specs=[
            pl.BlockSpec((rows * 4, 128), lambda i: (i, 0)),
            pl.BlockSpec((rows, 128), lambda i: (i, 0)),
        ]
        + [whole(s) for s, _ in outs[1:]],
        out_specs=[
            pl.BlockSpec((rows * 4, 128), lambda i: (i, 0)),
            whole((32, 64)),
            whole((4, 128)),
        ],
        compiler_params=pltpu.CompilerParams(vmem_limit_bytes=24 << 20),
        name="update",
    )(matrix.reshape(n_rows * 4, 128), *got)
    return (
        out.reshape(matrix.shape),
        r.reshape(row_weight.shape),
        c.reshape(column_weight.shape),
    )


def solution(mesh):
    return jax.shard_map(
        per_device,
        mesh=mesh,
        in_specs=(
            P(None, "col", None, None, "row", None),
            P(None, "row", None),
            P(None, "col", None),
        ),
        out_specs=(
            P(None, "col", None, None, "row", None),
            P(None, "col", None),
            P(None, "row", None),
        ),
        check_vma=False,
    )
```
